256 devices in a mesh: seq: 64 (over z, x, core), head: 4 (over y).
Axes of the slice: x: 4, y: 4, z: 8, core: 2. Of those that a mesh axis runs over, the one named last changes fastest.
Arguments:
- ssm_input: float32 [32768, 4096], P('seq', 'head'), may hold values from -50 to 50
- gate_input: bfloat16 [32768, 4096], P('seq', 'head'), may hold values from -6 to 6
- step_raw: float32 [32768, 64], P('seq', 'head'), may hold values from -6 to 65536
- decay_log: float32 [64], P('head')
- state_in: float32 [32768, 4, 128], P('seq', 'head'), may hold values from -0.5 to 0.5
- state_out: float32 [32768, 4, 128], P('seq', 'head'), may hold values from -6 to 6
- skip_gain: float32 [64], P('head'), may hold values from 0.5 to 2
- norm_gain: float32 [4096], P('head'), may hold values from 0.25 to 1.75
- out_weight: bfloat16 [4096, 4096], P('head'), may hold values from -0.09375 to 0.09375
Outputs:
- layer_out: bfloat16 [32768, 4096], P(('seq', 'head'))
The draws below stay inside these ranges and needn't reach their ends.
All inputs are finite; a program needn't handle non-finite values.
Results may differ from the reference program's by a relative error of at most 0.015.
Values may be sent and summed in bfloat16 or wider, within the bound.
A program may use at most 192 MiB of HBM per device.

```python
import math
import jax
import jax.numpy as jnp
from jax import lax

HEAD_COUNT = 64
P_SIZE = 64
N = 128
GROUPS = 4
DOUT = 4096
SPAN = 256
TOKENS = 32768


def spike_layout(key):
    base_offset = jax.random.fold_in(key, 9173)
    random_key_list = jax.random.split(base_offset, 5)
    pick = jax.random.uniform(random_key_list[0], (HEAD_COUNT,))
    fast_share = 0.4
    slow_rate = jnp.exp(jax.random.uniform(random_key_list[1], (HEAD_COUNT,), minval=math.log(0.5), maxval=math.log(5.0))) / TOKENS
    fast_rate = jnp.exp(jax.random.uniform(random_key_list[2], (HEAD_COUNT,), minval=math.log(1.0 / 3.0), maxval=0.0))
    rate_values = jnp.where(pick < fast_share, fast_rate, slow_rate)
    spots = jax.random.randint(random_key_list[3], (3,), 0, TOKENS)
    flagged_rows = jnp.any(jnp.arange(TOKENS)[:, None] == spots[None, :], axis=1)
    spike_increment = jax.random.uniform(random_key_list[4], (HEAD_COUNT,), minval=0.22, maxval=0.6) / rate_values
    return (rate_values, flagged_rows, spike_increment)


def draw_decay_log(key, part):
    rate_values, flagged_rows, spike_increment = spike_layout(key)
    return jnp.log(rate_values).astype(jnp.float32)


def draw_step_raw(key, part):
    rate_values, flagged_rows, spike_increment = spike_layout(key)
    noise_key = jax.random.fold_in(key, 31)
    base_offset = -3.0 + 0.7 * jnp.clip(jax.random.normal(noise_key, (TOKENS, HEAD_COUNT)), -4.0, 4.0)
    spike_unscaled = spike_increment + jnp.log(-jnp.expm1(-spike_increment))
    return jnp.where(flagged_rows[:, None], spike_unscaled[None, :], base_offset).astype(jnp.float32)


def draw_ssm_input(key, part):
    rate_values, flagged_rows, spike_increment = spike_layout(key)
    random_key_list = jax.random.split(jax.random.fold_in(key, 57), 3)
    values = jnp.clip(jax.random.normal(random_key_list[0], (TOKENS, HEAD_COUNT * P_SIZE)), -4.0, 4.0)
    half_range = 0.5 * math.log(10.0)
    row_scale = jnp.exp(jax.random.uniform(random_key_list[1], (TOKENS, 1), minval=-half_range, maxval=half_range))
    col_scale = jnp.exp(jax.random.uniform(random_key_list[2], (1, HEAD_COUNT * P_SIZE), minval=-half_range, maxval=half_range))
    attenuation = jnp.where(flagged_rows[:, None], 1.0 / spike_increment[None, :], 1.0)
    return (values * row_scale * col_scale * jnp.repeat(attenuation, P_SIZE, axis=1)).astype(jnp.float32)


def levels(key, shape, cuts, least, largest):
    def one(position, blocks):
        draws = jax.random.uniform(jax.random.fold_in(jax.random.fold_in(key, 6), position), (blocks,), jnp.float32, least / len(cuts), largest / len(cuts))
        return jnp.repeat(jnp.exp(draws), shape[position] // blocks).reshape((-1,) + (1,) * (len(shape) - position - 1))

    loudness = one(*cuts[0])
    for cut in cuts[1:]:
        loudness = loudness * one(*cut)
    return loudness


def bell_draw(key, dims, scale, bound, cuts=(), dtype=jnp.bfloat16):
    loudness = levels(key, dims, cuts, -0.22, 0.18) if cuts else 1.0
    values = jax.random.normal(key, dims, jnp.float32) * scale * loudness
    return jnp.minimum(jnp.maximum(values, -bound), bound).astype(dtype)


def setup_inputs(seed: int = 0) -> dict:
    key_of = jax.random.split(jax.random.key(seed), 10)
    return {
        "ssm_input": draw_ssm_input(jax.random.fold_in(key_of[9], 71), 0),
        "gate_input": bell_draw(key_of[1], (TOKENS, HEAD_COUNT * P_SIZE), 1.0, 6.0, ((0, 64), (1, 4))),
        "step_raw": draw_step_raw(jax.random.fold_in(key_of[9], 71), 0),
        "decay_log": draw_decay_log(jax.random.fold_in(key_of[9], 71), 0),
        "state_in": bell_draw(key_of[4], (TOKENS, GROUPS, N), N ** -0.5, 0.5, ((0, 64), (1, 4)), jnp.float32),
        "state_out": bell_draw(key_of[5], (TOKENS, GROUPS, N), 1.0, 6.0, ((0, 64), (1, 4)), jnp.float32),
        "skip_gain": jnp.clip(0.5 + 1.5 * jax.random.uniform(key_of[6], (HEAD_COUNT,), jnp.float32) ** levels(key_of[6], (HEAD_COUNT,), ((0, 4),), -0.2, 0.2), 0.5, 2.0),
        "norm_gain": jnp.clip(1.0 + 0.15 * jax.random.normal(key_of[7], (HEAD_COUNT * P_SIZE,), jnp.float32), 0.25, 1.75),
        "out_weight": bell_draw(key_of[8], (HEAD_COUNT * P_SIZE, DOUT), (HEAD_COUNT * P_SIZE) ** -0.5, 0.09375, ((0, 4),)),
    }


def span_pass(carry, blocks_in):
    exact = lax.Precision.HIGHEST
    inputs, steps_in, logs_in, in_rows, out_rows = blocks_in
    per_group = HEAD_COUNT // GROUPS
    cumulative = jnp.cumsum(logs_in, axis=0)
    across = jnp.transpose(cumulative, (1, 0))
    causal = jnp.arange(SPAN)[:, None] >= jnp.arange(SPAN)[None, :]
    decays_in = jnp.exp(jnp.where(causal[None], across[:, :, None] - across[:, None, :], -jnp.inf))
    scores = jnp.einsum('ign,jgn->gij', out_rows, in_rows, precision=exact)
    mixing = jnp.repeat(scores, per_group, axis=0) * decays_in
    weighted = inputs * steps_in[:, :, None]
    within = jnp.einsum('hij,jhp->ihp', mixing, weighted, precision=exact)
    in_heads = jnp.repeat(in_rows, per_group, axis=1)
    out_heads = jnp.repeat(out_rows, per_group, axis=1)
    carried = jnp.einsum('ihn,hpn->ihp', out_heads, carry, precision=exact) * jnp.exp(cumulative)[:, :, None]
    to_end = jnp.exp(cumulative[-1][None, :] - cumulative)
    added = jnp.einsum('jhp,jhn->hpn', weighted * to_end[:, :, None], in_heads, precision=exact)
    new_state = carry * jnp.exp(cumulative[-1])[:, None, None] + added
    return (new_state, within + carried)

def reference(ssm_input, gate_input, step_raw, decay_log, state_in, state_out, skip_gain, norm_gain, out_weight):
    span_count = TOKENS // SPAN
    step = jax.nn.softplus(step_raw)
    logdecay = -step * jnp.exp(decay_log)[None, :]
    blocks_all = (ssm_input.reshape(span_count, SPAN, HEAD_COUNT, P_SIZE), step.reshape(span_count, SPAN, HEAD_COUNT), logdecay.reshape(span_count, SPAN, HEAD_COUNT), state_in.reshape(span_count, SPAN, GROUPS, N), state_out.reshape(span_count, SPAN, GROUPS, N))
    start_state = jnp.zeros((HEAD_COUNT, P_SIZE, N), jnp.float32)
    _, outputs = lax.scan(span_pass, start_state, blocks_all)
    ssd = outputs.reshape(TOKENS, HEAD_COUNT, P_SIZE) + skip_gain[None, :, None] * ssm_input.reshape(TOKENS, HEAD_COUNT, P_SIZE)
    gated = ssd.reshape(TOKENS, HEAD_COUNT * P_SIZE) * jax.nn.silu(gate_input.astype(jnp.float32))
    grouped = gated.reshape(TOKENS, GROUPS, HEAD_COUNT * P_SIZE // GROUPS)
    scaled = grouped * lax.rsqrt(lax.optimization_barrier(jnp.mean(grouped * grouped, axis=2, keepdims=True)) + 1e-05)
    normed = (scaled.reshape(TOKENS, HEAD_COUNT * P_SIZE) * norm_gain[None, :]).astype(jnp.bfloat16)
    return jnp.dot(normed, out_weight, preferred_element_type=jnp.float32).astype(jnp.bfloat16)
```

```python
import functools

import jax
import jax.numpy as jnp
from jax import lax
from jax.experimental import pallas as pl
from jax.experimental.pallas import tpu as pltpu
from jax.sharding import PartitionSpec as P

F32, BF16 = jnp.float32, jnp.bfloat16
P_SIZE = 64
N = 128
BLOCK = 128
ROW = 8
PIECE = 512
LANES = 128
EXACT = lax.Precision.HIGHEST
MESH = pl.DeviceIdType.MESH


def dot(a, b):
    return jnp.dot(a, b, preferred_element_type=F32)


def exact_dot(a, b):
    return jnp.dot(a, b, preferred_element_type=F32, precision=EXACT)


def stack_rows(rows, count):
    where_row = lax.broadcasted_iota(jnp.int32, (count, rows[0].shape[1]), 0)
    out = jnp.zeros((count, rows[0].shape[1]), F32)
    for k, row in enumerate(rows):
        out = jnp.where(where_row == k, jnp.broadcast_to(row, out.shape), out)
    return out


def kernel(
    row_n, z_n, y_n,
    x_hbm, g_hbm, sr_hbm, dl_ref, b_hbm, c_hbm, sk_ref, ng_ref, w_hbm,
    o_hbm,
    xv, gv, srv, bv, cv, wv,
    spread, step_s, cum_s, cum_t, ecum_s, b_t, c_b,
    sent, lead, sbuf, rbuf, tbuf, ubuf, zs, zr, lt, lr, zt, zl, pre,
    yw, sg, nb, own,
    so, s_right, s_left, ro_left, ro_right, rf_left, rf_right, ob,
    in_sem, row_s, row_r, log_s, log_r, z_s, z_r, zlog_s, zlog_r, back_s, back_r, sum_s, sum_r, out_sem,
):
    tokens, width = xv.shape
    heads = srv.shape[1]
    blocks = tokens // BLOCK
    pieces = wv.shape[1] // PIECE
    half = pieces // 2
    me = lax.axis_index("seq")
    y = lax.axis_index("head")
    z, r = lax.div(me, row_n), lax.rem(me, row_n)
    right, left, opp = lax.rem(y + 1, y_n), lax.rem(y + y_n - 1, y_n), lax.rem(y + 2, y_n)

    def row_peer(j):
        return lax.rem(r + j, row_n)

    def z_peer(j):
        return lax.rem(z + j, z_n)

    barrier = pltpu.get_barrier_semaphore()
    for j in range(1, row_n):
        pl.semaphore_signal(barrier, inc=1, device_id=(z * row_n + row_peer(j), y), device_id_type=MESH)
    for j in range(1, z_n):
        pl.semaphore_signal(barrier, inc=1, device_id=(z_peer(j) * row_n + r, y), device_id_type=MESH)
    for side in (right, left):
        pl.semaphore_signal(barrier, inc=1, device_id=(me, side), device_id_type=MESH)

    loads = [
        pltpu.make_async_copy(src, dst, in_sem.at[k])
        for k, (src, dst) in enumerate(
            ((sr_hbm, srv), (b_hbm, bv), (x_hbm, xv), (c_hbm, cv), (g_hbm, gv), (w_hbm, wv))
        )
    ]
    for load in loads:
        load.start()

    head_of = lax.broadcasted_iota(jnp.int32, (heads, width), 1) // P_SIZE
    spread[...] = jnp.where(head_of == lax.broadcasted_iota(jnp.int32, (heads, width), 0), 1.0, 0.0).astype(BF16)

    def spread_rows(rows):
        return exact_dot(rows, spread[...].astype(F32))

    loads[0].wait()
    raw = srv[...]
    step = jnp.maximum(raw, 0.0) + jnp.log1p(jnp.exp(-jnp.abs(raw)))
    step_s[...] = step.astype(BF16)
    logdecay = -step * jnp.exp(dl_ref[...])
    row_i = lax.broadcasted_iota(jnp.int32, (BLOCK, BLOCK), 0)
    col_i = lax.broadcasted_iota(jnp.int32, (BLOCK, BLOCK), 1)
    lower = jnp.where(row_i >= col_i, 1.0, 0.0)
    totals, leads, ends = [], [], []
    so_far = jnp.zeros((1, heads), F32)
    for c in range(blocks):
        rows = slice(c * BLOCK, (c + 1) * BLOCK)
        cum = exact_dot(lower, logdecay[rows])
        cum_s[rows] = cum
        cum_t[c] = jnp.transpose(cum)
        ecum_s[rows] = jnp.exp(cum).astype(BF16)
        total = cum[BLOCK - 1 : BLOCK]
        ends.append((step[rows] * jnp.exp(total - cum)).astype(BF16))
        totals.append(total)
        leads.append(so_far)
        so_far = so_far + total
    lt[...] = jnp.zeros(lt.shape, F32)
    lt[:, 0:heads] = jnp.broadcast_to(so_far, (8, heads))
    factors = spread_rows(jnp.exp(stack_rows(totals + leads, 8)))
    for c in range(blocks):
        lead[c] = jnp.broadcast_to(factors[blocks + c : blocks + c + 1], (8, width))

    loads[1].wait()
    for c in range(blocks):
        b_t[c] = jnp.transpose(bv[c * BLOCK : (c + 1) * BLOCK, :]).astype(BF16)
    loads[2].wait()
    tile = 256
    for t in range(width // tile):
        lanes = slice(t * tile, (t + 1) * tile)
        state = jnp.zeros((N, tile), F32)
        for c in range(blocks):
            rows = slice(c * BLOCK, (c + 1) * BLOCK)
            sent[c, :, lanes] = state
            ended = (xv[rows, lanes] * dot(ends[c], spread[:, lanes])).astype(BF16)
            state = state * factors[c : c + 1, lanes] + dot(b_t[c], ended)
        sbuf[:, :, lanes] = state.astype(BF16).reshape(row_n, N // row_n, tile)

    pl.semaphore_wait(barrier, row_n - 1 + z_n - 1 + 2)

    def row_copies(j):
        k = row_peer(j)
        where = (z * row_n + k, y)
        return (
            pltpu.make_async_remote_copy(lt, lr.at[r], log_s.at[j], log_r.at[j], device_id=where, device_id_type=MESH),
            pltpu.make_async_remote_copy(
                sbuf.at[k], rbuf.at[r], row_s.at[j], row_r.at[j], device_id=where, device_id_type=MESH
            ),
        )

    for j in range(1, row_n):
        for copy in row_copies(j):
            copy.start()
    lr[r] = lt[...]
    rbuf[r] = sbuf[r]

    first_half = lax.broadcasted_iota(jnp.int32, (BLOCK, LANES), 1) < P_SIZE
    loads[3].wait()
    c_b[...] = cv[...].astype(BF16)
    loads[4].wait()
    skip = spread_rows(jnp.broadcast_to(sk_ref[...], (8, heads)))

    def within(c, carry):
        rows = pl.ds(pl.multiple_of(c * BLOCK, BLOCK), BLOCK)
        scores = jnp.where(row_i >= col_i, dot(c_b[rows, :], b_t[c]), 0.0)
        cum = cum_s[rows, :]
        across = cum_t[c]
        steps = step_s[rows, :]
        for pair in range(width // LANES):
            lanes = slice(pair * LANES, (pair + 1) * LANES)
            mixes = []
            for h in (2 * pair, 2 * pair + 1):
                gap = jnp.minimum(cum[:, h : h + 1] - across[h : h + 1, :], 0.0)
                mixes.append((scores * jnp.exp(gap)).astype(BF16))
            x = xv[rows, lanes]
            weighted = x * dot(steps, spread[:, lanes])
            both = jnp.concatenate(
                [jnp.where(first_half, weighted, 0.0), jnp.where(first_half, 0.0, weighted)], axis=0
            ).astype(BF16)
            yw[rows, lanes] = dot(jnp.concatenate(mixes, axis=1), both) + skip[0:1, lanes] * x
            gate = gv[rows, lanes].astype(F32)
            sg[rows, lanes] = gate / (1.0 + jnp.exp(-gate))
        return carry

    lax.fori_loop(0, blocks // 2, within, 0)

    for j in range(1, row_n):
        for copy in row_copies(j):
            copy.wait_recv()
    logs = [lr[k][0:1, 0:heads] for k in range(row_n)]
    ahead, running = [], jnp.zeros((1, heads), F32)
    for log in logs:
        ahead.append(running)
        running = running + log
    decay_row = spread_rows(jnp.exp(stack_rows(logs, 8)))
    ahead_row = spread_rows(jnp.exp(stack_rows(ahead, 8)))
    state = jnp.zeros((N // row_n, width), F32)
    for k in range(row_n):
        pre[k] = state
        state = state * decay_row[k : k + 1] + rbuf[k].astype(F32)
    zs[...] = state.astype(BF16)
    zt[...] = jnp.zeros(zt.shape, F32)
    zt[:, 0:heads] = jnp.broadcast_to(running, (8, heads))

    def z_copies(j):
        where = (z_peer(j) * row_n + r, y)
        return (
            pltpu.make_async_remote_copy(zt, zl.at[z], zlog_s.at[j], zlog_r.at[j], device_id=where, device_id_type=MESH),
            pltpu.make_async_remote_copy(zs, zr.at[z], z_s.at[j], z_r.at[j], device_id=where, device_id_type=MESH),
        )

    for j in range(1, z_n):
        for copy in z_copies(j):
            copy.start()
    zl[z] = zt[...]
    zr[z] = zs[...]

    lax.fori_loop(blocks // 2, blocks, within, 0)

    for j in range(1, z_n):
        for copy in z_copies(j):
            copy.wait_recv()
    decay_z = spread_rows(jnp.exp(stack_rows([zl[k][0:1, 0:heads] for k in range(z_n)], 8)))
    incoming = jnp.zeros((N // row_n, width), F32)
    for k in range(z_n - 1):
        incoming = jnp.where(k < z, incoming * decay_z[k : k + 1] + zr[k].astype(F32), incoming)
    for k in range(row_n):
        tbuf[k] = (pre[k] + incoming * ahead_row[k : k + 1]).astype(BF16)

    def back_copy(j):
        k = row_peer(j)
        return pltpu.make_async_remote_copy(
            tbuf.at[k], ubuf.at[r], back_s.at[j], back_r.at[j], device_id=(z * row_n + k, y), device_id_type=MESH
        )

    for j in range(1, row_n):
        back_copy(j).start()
    ubuf[r] = tbuf[r]
    loads[5].wait()
    for j in range(1, row_n):
        back_copy(j).wait_recv()

    def norm(d):
        rows = pl.ds(pl.multiple_of(d * BLOCK, BLOCK), BLOCK)
        led = lead[d]
        squares = jnp.zeros((BLOCK, 1), F32)
        c_rows = c_b[rows, :]
        decays = ecum_s[rows, :]
        for t in range(width // tile):
            lanes = slice(t * tile, (t + 1) * tile)
            came = ubuf[:, :, lanes].reshape(N, tile).astype(F32)
            entering = (sent[d, :, lanes] + led[0:1, lanes] * came).astype(BF16)
            ssd = yw[rows, lanes] + dot(c_rows, entering) * dot(decays, spread[:, lanes])
            gated = ssd * sg[rows, lanes]
            squares = squares + jnp.sum(gated * gated, axis=1, keepdims=True)
            sg[rows, lanes] = gated
        scale = lax.rsqrt(squares * (1.0 / width) + 1e-05)
        for t in range(width // tile):
            lanes = slice(t * tile, (t + 1) * tile)
            nb[rows, lanes] = (sg[rows, lanes] * scale * ng_ref[:, lanes]).astype(BF16)

    def product(d, p):
        rows = pl.ds(pl.multiple_of(d * BLOCK, BLOCK), BLOCK)
        return dot(nb[rows, :], wv[:, pl.ds(pl.multiple_of(p * PIECE, PIECE), PIECE)])

    def far_right(i):
        return pltpu.make_async_remote_copy(
            so.at[i], ro_left.at[i], sum_s.at[i], sum_r.at[i], device_id=(me, right), device_id_type=MESH
        )

    def far_left(i):
        return pltpu.make_async_remote_copy(
            so.at[half + i], ro_right.at[i], sum_s.at[half + i], sum_r.at[half + i],
            device_id=(me, left), device_id_type=MESH,
        )

    def to_right(p):
        return pltpu.make_async_remote_copy(
            s_right.at[p], rf_left.at[p], sum_s.at[pieces + p], sum_r.at[pieces + p],
            device_id=(me, right), device_id_type=MESH,
        )

    def to_left(p):
        return pltpu.make_async_remote_copy(
            s_left.at[p], rf_right.at[p], sum_s.at[2 * pieces + p], sum_r.at[2 * pieces + p],
            device_id=(me, left), device_id_type=MESH,
        )

    def out_copy(p):
        return pltpu.make_async_copy(
            ob.at[p], o_hbm.at[:, pl.ds(pl.multiple_of(p * PIECE, PIECE), PIECE)], out_sem.at[p]
        )

    norm(opp)

    def far_step(i, carry):
        so[i] = product(opp, i).astype(BF16)
        far_right(i).start()
        so[half + i] = product(opp, half + i).astype(BF16)
        far_left(i).start()
        return carry

    lax.fori_loop(0, half, far_step, 0)
    norm(right)
    norm(left)

    def near_step(i, carry):
        s_right[half + i] = product(right, half + i).astype(BF16)
        to_right(half + i).start()
        s_left[i] = product(left, i).astype(BF16)
        to_left(i).start()
        return carry

    lax.fori_loop(0, half, near_step, 0)
    norm(y)

    def own_step(p, carry):
        own[p] = product(y, p)
        return carry

    lax.fori_loop(0, pieces, own_step, 0)

    def sum_step(i, carry):
        ahead_right = product(right, i)
        ahead_left = product(left, half + i)
        far_right(i).wait_recv()
        s_right[i] = (ahead_right + ro_left[i].astype(F32)).astype(BF16)
        to_right(i).start()
        far_left(i).wait_recv()
        s_left[half + i] = (ahead_left + ro_right[i].astype(F32)).astype(BF16)
        to_left(half + i).start()
        return carry

    lax.fori_loop(0, half, sum_step, 0)

    def last_step(i, carry):
        for p in (i, half + i):
            to_right(p).wait_recv()
            to_left(p).wait_recv()
            ob[p] = (own[p] + rf_left[p].astype(F32) + rf_right[p].astype(F32)).astype(BF16)
            out_copy(p).start()
        return carry

    lax.fori_loop(0, half, last_step, 0)

    for j in range(1, row_n):
        for copy in row_copies(j):
            copy.wait_send()
        back_copy(j).wait_send()
    for j in range(1, z_n):
        for copy in z_copies(j):
            copy.wait_send()

    def drain(i, carry):
        far_right(i).wait_send()
        far_left(i).wait_send()
        for p in (i, half + i):
            to_right(p).wait_send()
            to_left(p).wait_send()
            out_copy(p).wait()
        return carry

    lax.fori_loop(0, half, drain, 0)


def solution(mesh):
    y_n = mesh.shape["head"]
    row_n = ROW
    z_n = mesh.shape["seq"] // row_n

    def per_device(x, g, sr, dl, b, c, sk, ng, w):
        tokens, width = x.shape
        heads = dl.shape[0]
        dout = w.shape[1]
        blocks = tokens // BLOCK
        pieces = dout // PIECE
        slab = N // row_n
        any_spec = pl.BlockSpec(memory_space=pl.ANY)
        vmem_spec = pl.BlockSpec(memory_space=pltpu.VMEM)
        dma = pltpu.SemaphoreType.DMA
        vmem = pltpu.VMEM
        half = (pieces // 2, BLOCK, PIECE)
        full = (pieces, BLOCK, PIECE)
        return pl.pallas_call(
            functools.partial(kernel, row_n, z_n, y_n),
            out_shape=jax.ShapeDtypeStruct((tokens // y_n, dout), BF16),
            in_specs=[any_spec] * 3 + [vmem_spec] + [any_spec] * 2 + [vmem_spec] * 2 + [any_spec],
            out_specs=any_spec,
            scratch_shapes=[
                vmem((tokens, width), F32), vmem((tokens, width), BF16), vmem((tokens, heads), F32),
                vmem((tokens, N), F32), vmem((tokens, N), F32), vmem(w.shape, BF16),
                vmem((heads, width), BF16), vmem((tokens, heads), BF16), vmem((tokens, heads), F32),
                vmem((blocks, heads, BLOCK), F32), vmem((tokens, heads), BF16),
                vmem((blocks, N, BLOCK), BF16), vmem((tokens, N), BF16),
                vmem((blocks, N, width), F32), vmem((blocks, 8, width), F32),
                vmem((row_n, slab, width), BF16), vmem((row_n, slab, width), BF16),
                vmem((row_n, slab, width), BF16), vmem((row_n, slab, width), BF16),
                vmem((slab, width), BF16), vmem((z_n, slab, width), BF16),
                vmem((8, LANES), F32), vmem((row_n, 8, LANES), F32),
                vmem((8, LANES), F32), vmem((z_n, 8, LANES), F32),
                vmem((row_n, slab, width), F32),
                vmem((tokens, width), F32), vmem((tokens, width), F32), vmem((tokens, width), BF16),
                vmem(full, F32),
                vmem(full, BF16), vmem(full, BF16), vmem(full, BF16),
                vmem(half, BF16), vmem(half, BF16), vmem(full, BF16), vmem(full, BF16), vmem(full, BF16),
                dma((6,)), dma((row_n,)), dma((row_n,)), dma((row_n,)), dma((row_n,)),
                dma((z_n,)), dma((z_n,)), dma((z_n,)), dma((z_n,)), dma((row_n,)), dma((row_n,)),
                dma((3 * pieces,)), dma((3 * pieces,)), dma((pieces,)),
            ],
            compiler_params=pltpu.CompilerParams(
                collective_id=0, has_side_effects=True, vmem_limit_bytes=60 * 1024 * 1024
            ),
        )(
            x, g, sr, dl.reshape(1, heads), b.reshape(tokens, N), c.reshape(tokens, N),
            sk.reshape(1, heads), ng.reshape(1, width), w,
        )

    in_specs = (
        P("seq", "head"), P("seq", "head"), P("seq", "head"), P("head"), P("seq", "head", None),
        P("seq", "head", None), P("head"), P("head"), P("head", None),
    )
    return jax.shard_map(
        per_device, mesh=mesh, in_specs=in_specs, out_specs=P(("seq", "head"), None), check_vma=False
    )
```

```python
import functools

import jax
import jax.numpy as jnp
from jax import lax
from jax.experimental import pallas as pl
from jax.experimental.pallas import tpu as pltpu
from jax.sharding import PartitionSpec as P

F32, BF16 = jnp.float32, jnp.bfloat16
P_SIZE = 64
N = 128
BLOCK = 128
CORES = 2
X = 4
ROW = CORES * X
GROUP = 4
PIECE = 512
LANES = 128
EXACT = lax.Precision.HIGHEST
MESH = pl.DeviceIdType.MESH


def dot(a, b):
    return jnp.dot(a, b, preferred_element_type=F32)


def exact_dot(a, b):
    return jnp.dot(a, b, preferred_element_type=F32, precision=EXACT)


def stack_rows(rows, count):
    where_row = lax.broadcasted_iota(jnp.int32, (count, rows[0].shape[1]), 0)
    out = jnp.zeros((count, rows[0].shape[1]), F32)
    for k, row in enumerate(rows):
        out = jnp.where(where_row == k, jnp.broadcast_to(row, out.shape), out)
    return out


def kernel(
    z_n, y_n,
    x_hbm, g_hbm, sr_hbm, dl_ref, b_hbm, c_hbm, sk_ref, ng_ref, w_hbm,
    ob,
    xv, gv, srv, bv, cv, wv,
    spread, spread_col, cum_t, cols_s, cols_b, b_t, c_b,
    sent, lead, sbuf, cbuf, xs, xr, bs, br, cs, ubuf, zs, zr, ps, pr,
    lt, cl, xt, xl, zt, zl, pre, zin,
    yw, sg, nb, own,
    so, s_right, s_left, ro_left, ro_right, rf_left, rf_right,
    in_sem, core_s, core_r, x_s, x_r, xlog_s, xlog_r, z_s, z_r, zlog_s, zlog_r, p_s, p_r, back_s, back_r, sum_s, sum_r,
):
    tokens, width = xv.shape
    heads = srv.shape[0]
    blocks = tokens // BLOCK
    pieces = wv.shape[1] // PIECE
    half = pieces // 2
    slab = N // ROW
    me = lax.axis_index("seq")
    y = lax.axis_index("head")
    z, r = lax.div(me, ROW), lax.rem(me, ROW)
    x_at, core = lax.div(r, CORES), lax.rem(r, CORES)
    z_in = lax.rem(z, GROUP)
    right, left, opp = lax.rem(y + 1, y_n), lax.rem(y + y_n - 1, y_n), lax.rem(y + 2, y_n)
    sibling = (me + 1 - 2 * core, y)
    gate_z = GROUP - 1

    def x_peer(j):
        return lax.rem(x_at + j, X)

    def at_x(k):
        return (z * ROW + k * CORES + core, y)

    def at_z(k):
        return (k * ROW + r, y)

    barrier = pltpu.get_barrier_semaphore()

    def greet(where):
        pl.semaphore_signal(barrier, inc=1, device_id=where, device_id_type=MESH)

    greet(sibling)
    for j in range(1, X):
        greet(at_x(x_peer(j)))
    greet((me, right))
    greet((me, left))
    for j in range(1, GROUP):
        pl.when(z_in >= j)(functools.partial(greet, at_z(z - j)))
    pl.when(z >= GROUP)(functools.partial(greet, at_z(gate_z)))

    loads = [
        pltpu.make_async_copy(src, dst, in_sem.at[k])
        for k, (src, dst) in enumerate(
            ((sr_hbm, srv), (b_hbm, bv), (x_hbm, xv), (c_hbm, cv), (g_hbm, gv), (w_hbm, wv))
        )
    ]
    for load in loads[:3]:
        load.start()

    head_of = lax.broadcasted_iota(jnp.int32, (heads, width), 1) // P_SIZE
    spread[...] = jnp.where(head_of == lax.broadcasted_iota(jnp.int32, (heads, width), 0), 1.0, 0.0).astype(BF16)
    spread_col[...] = jnp.zeros(spread_col.shape, BF16)
    for k in range(1, 4):
        spread_col[k, k * heads : (k + 1) * heads, :] = spread[...]

    def spread_rows(rows):
        high = rows.astype(BF16)
        return dot(high, spread[...]) + dot((rows - high.astype(F32)).astype(BF16), spread[...])

    def tile_of(row):
        return jnp.concatenate([row, jnp.zeros((1, LANES - heads), F32)], axis=1)

    loads[0].wait()
    rate = jnp.transpose(jnp.broadcast_to(jnp.exp(dl_ref[...]), (BLOCK, heads)))
    row_i = lax.broadcasted_iota(jnp.int32, (BLOCK, BLOCK), 0)
    col_i = lax.broadcasted_iota(jnp.int32, (BLOCK, BLOCK), 1)
    upper = jnp.where(row_i <= col_i, 1.0, 0.0)
    totals, leads = [], []
    so_far = jnp.zeros((1, heads), F32)
    for c in range(blocks):
        raw = srv[:, c * BLOCK : (c + 1) * BLOCK]
        step = jnp.maximum(raw, 0.0) + jnp.log1p(jnp.exp(-jnp.abs(raw)))
        cum = exact_dot(-step * rate, upper)
        cum_t[c] = cum
        to_end = step * jnp.exp(cum[:, BLOCK - 1 : BLOCK] - cum)
        cols = jnp.transpose(jnp.concatenate([cum, to_end, jnp.exp(cum), step], axis=0))
        cols_s[c] = cols
        cols_b[c] = cols.astype(BF16)
        total = cols[BLOCK - 1 : BLOCK, 0:heads]
        totals.append(total)
        leads.append(so_far)
        so_far = so_far + total
    lt[...] = jnp.zeros(lt.shape, F32)
    lt[:, 0:heads] = jnp.broadcast_to(so_far, (8, heads))
    factors = spread_rows(jnp.exp(stack_rows(totals + leads, 8)))
    for c in range(blocks):
        lead[c] = jnp.broadcast_to(factors[blocks + c : blocks + c + 1], (8, width))

    loads[1].wait()
    for c in range(blocks):
        b_t[c] = jnp.transpose(bv[c * BLOCK : (c + 1) * BLOCK, :]).astype(BF16)
    loads[2].wait()
    for load in loads[3:]:
        load.start()
    tile = 256
    for t in range(width // tile):
        lanes = slice(t * tile, (t + 1) * tile)
        state = jnp.zeros((N, tile), F32)
        for c in range(blocks):
            rows = slice(c * BLOCK, (c + 1) * BLOCK)
            sent[c, :, lanes] = state
            ended = (xv[rows, lanes] * dot(cols_b[c], spread_col[1, :, lanes])).astype(BF16)
            state = state * factors[c : c + 1, lanes] + dot(b_t[c], ended)
        sbuf[:, :, :, lanes] = state.astype(BF16).reshape(CORES, X, slab, tile)

    pl.semaphore_wait(barrier, X + 2 + (GROUP - 1 - z_in) + jnp.where(z == gate_z, z_n - GROUP, 0))

    core_log = pltpu.make_async_remote_copy(
        lt, cl.at[core], core_s.at[0], core_r.at[0], device_id=sibling, device_id_type=MESH
    )
    core_state = pltpu.make_async_remote_copy(
        sbuf.at[1 - core], cbuf.at[core], core_s.at[1], core_r.at[1], device_id=sibling, device_id_type=MESH
    )
    core_log.start()
    core_state.start()
    cl[core] = lt[...]
    cbuf[core] = sbuf[core]
    core_log.wait_recv()
    log_first, log_second = cl[0][0:1, 0:heads], cl[1][0:1, 0:heads]
    decay_core = spread_rows(jnp.exp(stack_rows([log_first, log_second], 8)))
    xt[...] = cl[0] + cl[1]
    core_state.wait_recv()
    for k in range(X):
        xs[k] = (cbuf[0, k].astype(F32) * decay_core[1:2] + cbuf[1, k].astype(F32)).astype(BF16)

    def x_copies(j):
        k = x_peer(j)
        return (
            pltpu.make_async_remote_copy(
                xt, xl.at[x_at], xlog_s.at[j], xlog_r.at[j], device_id=at_x(k), device_id_type=MESH
            ),
            pltpu.make_async_remote_copy(
                xs.at[k], xr.at[x_at], x_s.at[j], x_r.at[j], device_id=at_x(k), device_id_type=MESH
            ),
        )

    for j in (2, 1, 3):
        for copy in x_copies(j):
            copy.start()
    xl[x_at] = xt[...]
    xr[x_at] = xs[x_at]

    first_half = lax.broadcasted_iota(jnp.int32, (BLOCK, LANES), 1) < P_SIZE
    loads[3].wait()
    c_b[...] = cv[...].astype(BF16)
    loads[4].wait()
    skip = spread_rows(jnp.broadcast_to(sk_ref[...], (8, heads)))

    def within(c, carry):
        rows = pl.ds(pl.multiple_of(c * BLOCK, BLOCK), BLOCK)
        scores = jnp.where(row_i >= col_i, dot(c_b[rows, :], b_t[c]), 0.0)
        cum = cols_s[c]
        across = cum_t[c]
        cols = cols_b[c]
        for pair in range(width // LANES):
            lanes = slice(pair * LANES, (pair + 1) * LANES)
            mixes = []
            for h in (2 * pair, 2 * pair + 1):
                gap = jnp.minimum(cum[:, h : h + 1] - across[h : h + 1, :], 0.0)
                mixes.append((scores * jnp.exp(gap)).astype(BF16))
            x = xv[rows, lanes]
            weighted = x * dot(cols, spread_col[3, :, lanes])
            both = jnp.concatenate(
                [jnp.where(first_half, weighted, 0.0), jnp.where(first_half, 0.0, weighted)], axis=0
            ).astype(BF16)
            yw[rows, lanes] = dot(jnp.concatenate(mixes, axis=1), both) + skip[0:1, lanes] * x
            gate = gv[rows, lanes].astype(F32)
            sg[rows, lanes] = gate / (1.0 + jnp.exp(-gate))
        return carry

    lax.fori_loop(0, blocks - 1, within, 0)

    for j in range(1, X):
        for copy in x_copies(j):
            copy.wait_recv()
    logs = [xl[k][0:1, 0:heads] for k in range(X)]
    ahead, running = [], jnp.zeros((1, heads), F32)
    for log in logs:
        ahead.append(running)
        running = running + log
    decay_row = spread_rows(jnp.exp(stack_rows(logs + ahead, 8)))
    state = jnp.zeros((slab, width), F32)
    for k in range(X):
        pre[k] = state
        state = state * decay_row[k : k + 1] + xr[k].astype(F32)
    zs[...] = state.astype(BF16)
    zt[...] = jnp.zeros(zt.shape, F32)
    zt[:, 0:heads] = jnp.broadcast_to(running, (8, heads))

    def z_copies(j, to):
        return (
            pltpu.make_async_remote_copy(
                zt, zl.at[z_in], zlog_s.at[j], zlog_r.at[j], device_id=at_z(to), device_id_type=MESH
            ),
            pltpu.make_async_remote_copy(
                zs, zr.at[z_in], z_s.at[j], z_r.at[j], device_id=at_z(to), device_id_type=MESH
            ),
        )

    def z_send(j):
        for copy in z_copies(j, z + j):
            copy.start()

    def z_take(j):
        for copy in z_copies(j, z):
            copy.wait_recv()

    def z_sent(j):
        for copy in z_copies(j, z + j):
            copy.wait_send()

    for j in range(1, GROUP):
        pl.when(z_in + j < GROUP)(functools.partial(z_send, j))

    lax.fori_loop(blocks - 1, blocks, within, 0)

    for j in range(1, GROUP):
        pl.when(z_in >= j)(functools.partial(z_take, j))
    logs, before = [], jnp.zeros((1, heads), F32)
    for k in range(GROUP - 1):
        log = jnp.where(k < z_in, zl[k][0:1, 0:heads], 0.0)
        logs.append(log)
        before = before + log
    decay_z = spread_rows(jnp.exp(stack_rows(logs + [before, running], 8)))
    zin[...] = jnp.zeros(zin.shape, F32)
    for k in range(GROUP - 1):

        @pl.when(k < z_in)
        def _(k=k):
            zin[...] = zin[...] * decay_z[k : k + 1] + zr[k].astype(F32)

    def gate_copy(j, to):
        return pltpu.make_async_remote_copy(ps, pr, p_s.at[j], p_r.at[0], device_id=at_z(to), device_id_type=MESH)

    @pl.when(z == gate_z)
    def _():
        ps[...] = (zin[...] * decay_z[GROUP : GROUP + 1] + state).astype(BF16)
        for j in range(z_n - GROUP):
            gate_copy(j, GROUP + j).start()

    @pl.when(z >= GROUP)
    def _():
        gate_copy(0, z).wait_recv()
        zin[...] = zin[...] + pr[...].astype(F32) * decay_z[GROUP - 1 : GROUP]

    for k in range(X):
        bs[k] = (pre[k] + zin[...] * decay_row[X + k : X + k + 1]).astype(BF16)

    def back_copy(j):
        k = x_peer(j)
        return pltpu.make_async_remote_copy(
            bs.at[k], br.at[x_at], back_s.at[j], back_r.at[j], device_id=at_x(k), device_id_type=MESH
        )

    for j in (2, 1, 3):
        back_copy(j).start()
    br[x_at] = bs[x_at]
    loads[5].wait()
    for j in range(1, X):
        back_copy(j).wait_recv()
    for k in range(X):
        came = br[k]
        passed = (came.astype(F32) * decay_core[0:1] + cbuf[0, k].astype(F32)).astype(BF16)
        cs[k] = jnp.where(core == 0, passed, came)
        ubuf[core, k] = jnp.where(core == 0, came, passed)
    core_back = pltpu.make_async_remote_copy(
        cs, ubuf.at[core], core_s.at[2], core_r.at[2], device_id=sibling, device_id_type=MESH
    )
    core_back.start()
    core_back.wait_recv()

    def norm(d):
        rows = pl.ds(pl.multiple_of(d * BLOCK, BLOCK), BLOCK)
        led = lead[d]
        squares = jnp.zeros((BLOCK, 1), F32)
        c_rows = c_b[rows, :]
        cols = cols_b[d]
        for t in range(width // tile):
            lanes = slice(t * tile, (t + 1) * tile)
            came = ubuf[:, :, :, lanes].reshape(N, tile).astype(F32)
            entering = (sent[d, :, lanes] + led[0:1, lanes] * came).astype(BF16)
            ssd = yw[rows, lanes] + dot(c_rows, entering) * dot(cols, spread_col[2, :, lanes])
            gated = ssd * sg[rows, lanes]
            squares = squares + jnp.sum(gated * gated, axis=1, keepdims=True)
            sg[rows, lanes] = gated
        scale = lax.rsqrt(squares * (1.0 / width) + 1e-05)
        for t in range(width // tile):
            lanes = slice(t * tile, (t + 1) * tile)
            nb[rows, lanes] = (sg[rows, lanes] * scale * ng_ref[:, lanes]).astype(BF16)

    def product(d, p):
        rows = pl.ds(pl.multiple_of(d * BLOCK, BLOCK), BLOCK)
        return dot(nb[rows, :], wv[:, pl.ds(pl.multiple_of(p * PIECE, PIECE), PIECE)])

    def far_right(i):
        return pltpu.make_async_remote_copy(
            so.at[i], ro_left.at[i], sum_s.at[i], sum_r.at[i], device_id=(me, right), device_id_type=MESH
        )

    def far_left(i):
        return pltpu.make_async_remote_copy(
            so.at[half + i], ro_right.at[i], sum_s.at[half + i], sum_r.at[half + i],
            device_id=(me, left), device_id_type=MESH,
        )

    def to_right(p):
        return pltpu.make_async_remote_copy(
            s_right.at[p], rf_left.at[p], sum_s.at[pieces + p], sum_r.at[pieces + p],
            device_id=(me, right), device_id_type=MESH,
        )

    def to_left(p):
        return pltpu.make_async_remote_copy(
            s_left.at[p], rf_right.at[p], sum_s.at[2 * pieces + p], sum_r.at[2 * pieces + p],
            device_id=(me, left), device_id_type=MESH,
        )

    norm(opp)

    def far_step(i, carry):
        so[i] = product(opp, i).astype(BF16)
        far_right(i).start()
        so[half + i] = product(opp, half + i).astype(BF16)
        far_left(i).start()
        return carry

    lax.fori_loop(0, half, far_step, 0)
    norm(right)
    norm(left)

    def near_step(i, carry):
        s_right[half + i] = product(right, half + i).astype(BF16)
        to_right(half + i).start()
        s_left[i] = product(left, i).astype(BF16)
        to_left(i).start()
        return carry

    lax.fori_loop(0, half, near_step, 0)
    norm(y)

    def own_step(p, carry):
        own[p] = product(y, p)
        return carry

    lax.fori_loop(0, pieces, own_step, 0)

    def sum_step(i, carry):
        ahead_right = product(right, i)
        ahead_left = product(left, half + i)
        far_right(i).wait_recv()
        s_right[i] = (ahead_right + ro_left[i].astype(F32)).astype(BF16)
        to_right(i).start()
        far_left(i).wait_recv()
        s_left[half + i] = (ahead_left + ro_right[i].astype(F32)).astype(BF16)
        to_left(half + i).start()
        return carry

    lax.fori_loop(0, half, sum_step, 0)

    def last_step(i, carry):
        for p in (i, half + i):
            to_right(p).wait_recv()
            to_left(p).wait_recv()
            ob[:, pl.ds(pl.multiple_of(p * PIECE, PIECE), PIECE)] = (
                own[p] + rf_left[p].astype(F32) + rf_right[p].astype(F32)
            ).astype(BF16)
        return carry

    lax.fori_loop(0, half, last_step, 0)

    for copy in (core_log, core_state, core_back):
        copy.wait_send()
    for j in range(1, X):
        for copy in x_copies(j):
            copy.wait_send()
        back_copy(j).wait_send()
    for j in range(1, GROUP):
        pl.when(z_in + j < GROUP)(functools.partial(z_sent, j))

    @pl.when(z == gate_z)
    def _():
        for j in range(z_n - GROUP):
            gate_copy(j, GROUP + j).wait_send()

    def drain(i, carry):
        far_right(i).wait_send()
        far_left(i).wait_send()
        for p in (i, half + i):
            to_right(p).wait_send()
            to_left(p).wait_send()
        return carry

    lax.fori_loop(0, half, drain, 0)


def solution(mesh):
    y_n = mesh.shape["head"]
    z_n = mesh.shape["seq"] // ROW

    def per_device(x, g, sr, dl, b, c, sk, ng, w):
        tokens, width = x.shape
        heads = dl.shape[0]
        dout = w.shape[1]
        blocks = tokens // BLOCK
        pieces = dout // PIECE
        slab = N // ROW
        hbm_spec = pl.BlockSpec(memory_space=pltpu.HBM)
        vmem_spec = pl.BlockSpec(memory_space=pltpu.VMEM)
        dma = pltpu.SemaphoreType.DMA
        vmem = pltpu.VMEM
        half = (pieces // 2, BLOCK, PIECE)
        full = (pieces, BLOCK, PIECE)
        rows = (X, slab, width)
        log = (8, LANES)
        return pl.pallas_call(
            functools.partial(kernel, z_n, y_n),
            out_shape=jax.ShapeDtypeStruct((tokens // y_n, dout), BF16),
            in_specs=[hbm_spec] * 3 + [vmem_spec] + [hbm_spec] * 2 + [vmem_spec] * 2 + [hbm_spec],
            out_specs=vmem_spec,
            scratch_shapes=[
                vmem((tokens, width), F32), vmem((tokens, width), BF16), vmem((heads, tokens), F32),
                vmem((tokens, N), F32), vmem((tokens, N), F32), vmem(w.shape, BF16),
                vmem((heads, width), BF16), vmem((4, 4 * heads, width), BF16), vmem((blocks, heads, BLOCK), F32),
                vmem((blocks, BLOCK, 4 * heads), F32), vmem((blocks, BLOCK, 4 * heads), BF16),
                vmem((blocks, N, BLOCK), BF16), vmem((tokens, N), BF16),
                vmem((blocks, N, width), F32), vmem((blocks, 8, width), F32),
                vmem((CORES,) + rows, BF16), vmem((CORES,) + rows, BF16),
                vmem(rows, BF16), vmem(rows, BF16), vmem(rows, BF16), vmem(rows, BF16), vmem(rows, BF16),
                vmem((CORES,) + rows, BF16),
                vmem((slab, width), BF16), vmem((GROUP, slab, width), BF16),
                vmem((slab, width), BF16), vmem((slab, width), BF16),
                vmem(log, F32), vmem((CORES,) + log, F32), vmem(log, F32), vmem((X,) + log, F32),
                vmem(log, F32), vmem((GROUP,) + log, F32), vmem(rows, F32), vmem((slab, width), F32),
                vmem((tokens, width), F32), vmem((tokens, width), F32), vmem((tokens, width), BF16),
                vmem(full, F32),
                vmem(full, BF16), vmem(full, BF16), vmem(full, BF16),
                vmem(half, BF16), vmem(half, BF16), vmem(full, BF16), vmem(full, BF16),
                dma((6,)), dma((3,)), dma((3,)), dma((X,)), dma((X,)), dma((X,)), dma((X,)),
                dma((GROUP,)), dma((GROUP,)), dma((GROUP,)), dma((GROUP,)),
                dma((z_n - GROUP,)), dma((1,)), dma((X,)), dma((X,)),
                dma((3 * pieces,)), dma((3 * pieces,)),
            ],
            compiler_params=pltpu.CompilerParams(
                collective_id=0, has_side_effects=True, vmem_limit_bytes=58 * 1024 * 1024
            ),
        )(
            x, g, sr.T, dl.reshape(1, heads), b.reshape(tokens, N), c.reshape(tokens, N),
            sk.reshape(1, heads), ng.reshape(1, width), w,
        )

    in_specs = (
        P("seq", "head"), P("seq", "head"), P("seq", "head"), P("head"), P("seq", "head", None),
        P("seq", "head", None), P("head"), P("head"), P("head", None),
    )
    return jax.shard_map(
        per_device, mesh=mesh, in_specs=in_specs, out_specs=P(("seq", "head"), None), check_vma=False
    )
```

```python
import functools

import jax
import jax.numpy as jnp
from jax import lax
from jax.experimental import pallas as pl
from jax.experimental.pallas import tpu as pltpu
from jax.sharding import PartitionSpec as P

F32, BF16 = jnp.float32, jnp.bfloat16
P_SIZE = 64
N = 128
BLOCK = 128
CORES = 2
X = 4
ROW = CORES * X
GROUP = 4
CHUNKS = 3
RING = 7
FAR_A = 4
PIECE = 256
LANES = 128
EXACT = lax.Precision.HIGHEST
MESH = pl.DeviceIdType.MESH


def dot(a, b):
    return jnp.dot(a, b, preferred_element_type=F32)


def exact_dot(a, b):
    return jnp.dot(a, b, preferred_element_type=F32, precision=EXACT)


def stack_rows(rows, count):
    where_row = lax.broadcasted_iota(jnp.int32, (count, rows[0].shape[1]), 0)
    out = jnp.zeros((count, rows[0].shape[1]), F32)
    for k, row in enumerate(rows):
        out = jnp.where(where_row == k, jnp.broadcast_to(row, out.shape), out)
    return out


def kernel(
    z_n, y_n,
    x_hbm, g_hbm, sr_hbm, dl_ref, b_hbm, c_hbm, sk_ref, ng_ref, w_hbm,
    ob,
    xv, gv, srv, bv, cv, wv,
    spread, spread_col, cum_t, cols_s, cols_b, b_t, c_b,
    sent, lead, sbuf, cbuf, xs, xr, bs, br, cs, ubuf, zs, zr, ps, pr,
    lt, cl, xt, xl, zt, zl, pre, zin,
    yw, sg, nl, na, nq, own_r, own_p,
    so, s_a, s_b, ro, rf_a, rf_b, pb, rb, wp,
    in_sem, core_s, core_r, x_s, x_r, xlog_s, xlog_r, z_s, z_r, zlog_s, zlog_r, p_s, p_r, back_s, back_r, sum_s, sum_r,
    n_s, n_r, pair_s, pair_r, wa_s, wa_r, wx_s, wx_r, ws_s, ws_r,
):
    tokens, width = xv.shape
    heads = srv.shape[0]
    blocks = tokens // BLOCK
    slab = N // ROW
    me = lax.axis_index("seq")
    y = lax.axis_index("head")
    z, r = lax.div(me, ROW), lax.rem(me, ROW)
    x_at, core = lax.div(r, CORES), lax.rem(r, CORES)
    z_in = lax.rem(z, GROUP)
    a_at, b_at, opp = y + 1 - 2 * lax.rem(y, 2), y_n - 1 - y, lax.rem(y + 2, y_n)
    sibling = (me + 1 - 2 * core, y)
    gate_z = GROUP - 1

    def x_peer(j):
        return lax.rem(x_at + j, X)

    def at_x(k):
        return (z * ROW + k * CORES + core, y)

    def at_z(k):
        return (k * ROW + r, y)

    barrier = pltpu.get_barrier_semaphore()

    def greet(where):
        pl.semaphore_signal(barrier, inc=1, device_id=where, device_id_type=MESH)

    greet(sibling)
    for j in range(1, X):
        greet(at_x(x_peer(j)))
    greet((me, a_at))
    greet((me, b_at))
    for j in range(1, GROUP):
        pl.when(z_in >= j)(functools.partial(greet, at_z(z - j)))
    pl.when(z >= GROUP)(functools.partial(greet, at_z(gate_z)))

    loads = [
        pltpu.make_async_copy(src, dst, in_sem.at[k])
        for k, (src, dst) in enumerate(
            ((sr_hbm, srv), (b_hbm, bv), (x_hbm, xv), (c_hbm, cv), (g_hbm, gv), (w_hbm, wv))
        )
    ]
    for load in loads[:3]:
        load.start()

    head_of = lax.broadcasted_iota(jnp.int32, (heads, width), 1) // P_SIZE
    spread[...] = jnp.where(head_of == lax.broadcasted_iota(jnp.int32, (heads, width), 0), 1.0, 0.0).astype(BF16)
    spread_col[...] = jnp.zeros(spread_col.shape, BF16)
    for k in range(1, 4):
        spread_col[k, k * heads : (k + 1) * heads, :] = spread[...]

    def spread_rows(rows):
        high = rows.astype(BF16)
        return dot(high, spread[...]) + dot((rows - high.astype(F32)).astype(BF16), spread[...])

    def tile_of(row):
        return jnp.concatenate([row, jnp.zeros((1, LANES - heads), F32)], axis=1)

    loads[0].wait()
    rate = jnp.transpose(jnp.broadcast_to(jnp.exp(dl_ref[...]), (BLOCK, heads)))
    row_i = lax.broadcasted_iota(jnp.int32, (BLOCK, BLOCK), 0)
    col_i = lax.broadcasted_iota(jnp.int32, (BLOCK, BLOCK), 1)
    upper = jnp.where(row_i <= col_i, 1.0, 0.0)
    totals, leads = [], []
    so_far = jnp.zeros((1, heads), F32)
    for c in range(blocks):
        raw = srv[:, c * BLOCK : (c + 1) * BLOCK]
        step = jnp.maximum(raw, 0.0) + jnp.log1p(jnp.exp(-jnp.abs(raw)))
        cum = exact_dot(-step * rate, upper)
        cum_t[c] = cum
        to_end = step * jnp.exp(cum[:, BLOCK - 1 : BLOCK] - cum)
        cols = jnp.transpose(jnp.concatenate([cum, to_end, jnp.exp(cum), step], axis=0))
        cols_s[c] = cols
        cols_b[c] = cols.astype(BF16)
        total = cols[BLOCK - 1 : BLOCK, 0:heads]
        totals.append(total)
        leads.append(so_far)
        so_far = so_far + total
    lt[...] = jnp.zeros(lt.shape, F32)
    lt[:, 0:heads] = jnp.broadcast_to(so_far, (8, heads))
    factors = spread_rows(jnp.exp(stack_rows(totals + leads, 8)))
    for c in range(blocks):
        lead[c] = jnp.broadcast_to(factors[blocks + c : blocks + c + 1], (8, width))

    loads[1].wait()
    for c in range(blocks):
        b_t[c] = jnp.transpose(bv[c * BLOCK : (c + 1) * BLOCK, :]).astype(BF16)
    loads[2].wait()
    for load in loads[3:]:
        load.start()
    pl.semaphore_wait(barrier, X + 2 + (GROUP - 1 - z_in) + jnp.where(z == gate_z, z_n - GROUP, 0))

    up, down = x_peer(1), x_peer(X - 1)
    near_piece = CORES * x_at + core

    def column(piece, k):
        quarter = lax.div(piece, CORES) * (wv.shape[1] // X)
        return pl.multiple_of(quarter + lax.rem(piece, CORES) * CHUNKS * LANES + k * LANES, LANES)

    def w_first(k):
        return pltpu.make_async_remote_copy(
            w_hbm.at[:, pl.ds(column(near_piece, k), LANES)], wp.at[near_piece, k], wa_s.at[k], wa_r.at[k],
            device_id=(me, a_at), device_id_type=MESH,
        )

    def w_beside(side, k):
        return pltpu.make_async_remote_copy(
            wp.at[near_piece, k], wp.at[near_piece, k], wx_s.at[side * CHUNKS + k], wx_r.at[side * CHUNKS + k],
            device_id=at_x(up if side == 0 else down), device_id_type=MESH,
        )

    def w_sibling(source, k):
        piece = CORES * (x_at, down, up)[source] + core
        return pltpu.make_async_remote_copy(
            wp.at[piece, k], wp.at[piece, k], ws_s.at[source * CHUNKS + k], ws_r.at[source * CHUNKS + k],
            device_id=sibling, device_id_type=MESH,
        )

    def w_pass(k):
        w_first(k).wait_recv()
        w_beside(0, k).start()
        w_beside(1, k).start()
        w_sibling(0, k).start()

    for k in range(CHUNKS):
        w_first(k).start()

    tile = 256
    for t in range(width // tile):
        lanes = slice(t * tile, (t + 1) * tile)
        state = jnp.zeros((N, tile), F32)
        for c in range(blocks):
            rows = slice(c * BLOCK, (c + 1) * BLOCK)
            sent[c, :, lanes] = state
            ended = (xv[rows, lanes] * dot(cols_b[c], spread_col[1, :, lanes])).astype(BF16)
            state = state * factors[c : c + 1, lanes] + dot(b_t[c], ended)
        sbuf[:, :, :, lanes] = state.astype(BF16).reshape(CORES, X, slab, tile)

    core_log = pltpu.make_async_remote_copy(
        lt, cl.at[core], core_s.at[0], core_r.at[0], device_id=sibling, device_id_type=MESH
    )
    core_state = pltpu.make_async_remote_copy(
        sbuf.at[1 - core], cbuf.at[core], core_s.at[1], core_r.at[1], device_id=sibling, device_id_type=MESH
    )
    core_log.start()
    core_state.start()
    cl[core] = lt[...]
    cbuf[core] = sbuf[core]
    core_log.wait_recv()
    log_first, log_second = cl[0][0:1, 0:heads], cl[1][0:1, 0:heads]
    decay_core = spread_rows(jnp.exp(stack_rows([log_first, log_second], 8)))
    xt[...] = cl[0] + cl[1]
    core_state.wait_recv()
    for k in range(X):
        xs[k] = (cbuf[0, k].astype(F32) * decay_core[1:2] + cbuf[1, k].astype(F32)).astype(BF16)

    def x_copies(j):
        k = x_peer(j)
        return (
            pltpu.make_async_remote_copy(
                xt, xl.at[x_at], xlog_s.at[j], xlog_r.at[j], device_id=at_x(k), device_id_type=MESH
            ),
            pltpu.make_async_remote_copy(
                xs.at[k], xr.at[x_at], x_s.at[j], x_r.at[j], device_id=at_x(k), device_id_type=MESH
            ),
        )

    for j in (2, 1, 3):
        for copy in x_copies(j):
            copy.start()
    xl[x_at] = xt[...]
    xr[x_at] = xs[x_at]

    first_half = lax.broadcasted_iota(jnp.int32, (BLOCK, LANES), 1) < P_SIZE
    loads[3].wait()
    c_b[...] = cv[...].astype(BF16)
    loads[4].wait()
    skip = spread_rows(jnp.broadcast_to(sk_ref[...], (8, heads)))

    def within(c, carry):
        rows = pl.ds(pl.multiple_of(c * BLOCK, BLOCK), BLOCK)
        scores = jnp.where(row_i >= col_i, dot(c_b[rows, :], b_t[c]), 0.0)
        cum = cols_s[c]
        across = cum_t[c]
        cols = cols_b[c]
        for pair in range(width // LANES):
            lanes = slice(pair * LANES, (pair + 1) * LANES)
            mixes = []
            for h in (2 * pair, 2 * pair + 1):
                gap = jnp.minimum(cum[:, h : h + 1] - across[h : h + 1, :], 0.0)
                mixes.append((scores * jnp.exp(gap)).astype(BF16))
            x = xv[rows, lanes]
            weighted = x * dot(cols, spread_col[3, :, lanes])
            both = jnp.concatenate(
                [jnp.where(first_half, weighted, 0.0), jnp.where(first_half, 0.0, weighted)], axis=0
            ).astype(BF16)
            yw[rows, lanes] = dot(jnp.concatenate(mixes, axis=1), both) + skip[0:1, lanes] * x
            gate = gv[rows, lanes].astype(F32)
            sg[rows, lanes] = gate / (1.0 + jnp.exp(-gate))
        return carry

    lax.fori_loop(0, blocks - 1, within, 0)

    for j in range(1, X):
        for copy in x_copies(j):
            copy.wait_recv()
    logs = [xl[k][0:1, 0:heads] for k in range(X)]
    ahead, running = [], jnp.zeros((1, heads), F32)
    for log in logs:
        ahead.append(running)
        running = running + log
    decay_row = spread_rows(jnp.exp(stack_rows(logs + ahead, 8)))
    state = jnp.zeros((slab, width), F32)
    for k in range(X):
        pre[k] = state
        state = state * decay_row[k : k + 1] + xr[k].astype(F32)
    zs[...] = state.astype(BF16)
    zt[...] = jnp.zeros(zt.shape, F32)
    zt[:, 0:heads] = jnp.broadcast_to(running, (8, heads))

    def z_copies(j, to):
        return (
            pltpu.make_async_remote_copy(
                zt, zl.at[z_in], zlog_s.at[j], zlog_r.at[j], device_id=at_z(to), device_id_type=MESH
            ),
            pltpu.make_async_remote_copy(
                zs, zr.at[z_in], z_s.at[j], z_r.at[j], device_id=at_z(to), device_id_type=MESH
            ),
        )

    def z_send(j):
        for copy in z_copies(j, z + j):
            copy.start()

    def z_take(j):
        for copy in z_copies(j, z):
            copy.wait_recv()

    def z_sent(j):
        for copy in z_copies(j, z + j):
            copy.wait_send()

    for j in range(1, GROUP):
        pl.when(z_in + j < GROUP)(functools.partial(z_send, j))

    def join_z():
        for j in range(1, GROUP):
            pl.when(z_in >= j)(functools.partial(z_take, j))
        logs, before = [], jnp.zeros((1, heads), F32)
        for k in range(GROUP - 1):
            log = jnp.where(k < z_in, zl[k][0:1, 0:heads], 0.0)
            logs.append(log)
            before = before + log
        decay_z = spread_rows(jnp.exp(stack_rows(logs + [before, running], 8)))
        zin[...] = jnp.zeros(zin.shape, F32)
        for k in range(GROUP - 1):

            @pl.when(k < z_in)
            def _(k=k):
                zin[...] = zin[...] * decay_z[k : k + 1] + zr[k].astype(F32)

        return decay_z

    def gate_copy(j, to):
        return pltpu.make_async_remote_copy(ps, pr, p_s.at[j], p_r.at[0], device_id=at_z(to), device_id_type=MESH)

    @pl.when(z == gate_z)
    def _():
        decay_z = join_z()
        ps[...] = (zin[...] * decay_z[GROUP : GROUP + 1] + state).astype(BF16)
        for j in range(z_n - GROUP - 1, -1, -1):
            gate_copy(j, GROUP + j).start()

    lax.fori_loop(blocks - 1, blocks, within, 0)

    @pl.when(z != gate_z)
    def _():
        decay_z = join_z()

        @pl.when(z >= GROUP)
        def _():
            gate_copy(0, z).wait_recv()
            zin[...] = zin[...] + pr[...].astype(F32) * decay_z[GROUP - 1 : GROUP]

    for k in range(X):
        bs[k] = (pre[k] + zin[...] * decay_row[X + k : X + k + 1]).astype(BF16)

    def back_copy(j):
        k = x_peer(j)
        return pltpu.make_async_remote_copy(
            bs.at[k], br.at[x_at], back_s.at[j], back_r.at[j], device_id=at_x(k), device_id_type=MESH
        )

    def core_back(j):
        k = lax.rem(x_at + X - j, X)
        return pltpu.make_async_remote_copy(
            cs.at[k], ubuf.at[core, k], core_s.at[2 + j], core_r.at[2 + j], device_id=sibling, device_id_type=MESH
        )

    for j in (2, 1, 3):
        back_copy(j).start()
    br[x_at] = bs[x_at]
    loads[5].wait()
    for j in (0, 1, 3, 2):
        if j:
            back_copy(j).wait_recv()
        k = lax.rem(x_at + X - j, X)
        came = br[k]
        passed = (came.astype(F32) * decay_core[0:1] + cbuf[0, k].astype(F32)).astype(BF16)
        cs[k] = jnp.where(core == 0, passed, came)
        ubuf[core, k] = jnp.where(core == 0, came, passed)
        core_back(j).start()
    for j in range(X):
        core_back(j).wait_recv()

    def norm(d, into, at):
        rows = pl.ds(pl.multiple_of(d * BLOCK, BLOCK), BLOCK)
        led = lead[d]
        squares = jnp.zeros((BLOCK, 1), F32)
        c_rows = c_b[rows, :]
        cols = cols_b[d]
        for t in range(width // tile):
            lanes = slice(t * tile, (t + 1) * tile)
            came = ubuf[:, :, :, lanes].reshape(N, tile).astype(F32)
            entering = (sent[d, :, lanes] + led[0:1, lanes] * came).astype(BF16)
            ssd = yw[rows, lanes] + dot(c_rows, entering) * dot(cols, spread_col[2, :, lanes])
            gated = ssd * sg[rows, lanes]
            squares = squares + jnp.sum(gated * gated, axis=1, keepdims=True)
            sg[rows, lanes] = gated
        scale = lax.rsqrt(squares * (1.0 / width) + 1e-05)
        for t in range(width // tile):
            lanes = slice(t * tile, (t + 1) * tile)
            into[at : at + BLOCK, lanes] = (sg[rows, lanes] * scale * ng_ref[:, lanes]).astype(BF16)

    def ring_columns(i):
        quarter = wv.shape[1] // X
        if i < X:
            start = x_peer(2) * quarter + i * PIECE
        else:
            start = x_peer((0, 1, X - 1)[i - X]) * quarter + CORES * CHUNKS * LANES
        return pl.ds(pl.multiple_of(start, PIECE), PIECE)

    def product(of, at, i):
        return dot(of[at : at + BLOCK, :], wv[:, ring_columns(i)])

    def far(i):
        return pltpu.make_async_remote_copy(
            so.at[i], ro.at[i], sum_s.at[i], sum_r.at[i],
            device_id=(me, a_at if i < FAR_A else b_at), device_id_type=MESH,
        )

    def to_a(i):
        return pltpu.make_async_remote_copy(
            s_a.at[i], rf_a.at[i], sum_s.at[RING + i], sum_r.at[RING + i], device_id=(me, a_at), device_id_type=MESH
        )

    def to_b(i):
        return pltpu.make_async_remote_copy(
            s_b.at[i], rf_b.at[i], sum_s.at[2 * RING + i], sum_r.at[2 * RING + i],
            device_id=(me, b_at), device_id_type=MESH,
        )

    def n_copy(i):
        rows = slice(i * BLOCK, (i + 1) * BLOCK)
        return pltpu.make_async_remote_copy(
            na.at[rows, :], nq.at[rows, :], n_s.at[i], n_r.at[i], device_id=(me, a_at), device_id_type=MESH
        )

    def pair_copy(piece, k):
        where = piece * CHUNKS + k
        return pltpu.make_async_remote_copy(
            pb.at[piece, k], rb.at[piece, k], pair_s.at[where], pair_r.at[where],
            device_id=(me, b_at), device_id_type=MESH,
        )

    def pair(rows, piece, k):
        columns = pl.ds(column(piece, k), LANES)
        return dot(nl[rows, :], wv[:, columns]) + dot(nq[rows, :], wp[piece, k])

    b_rows, own_rows, both_rows = slice(0, BLOCK), slice(BLOCK, 2 * BLOCK), slice(0, 2 * BLOCK)

    def pair_b(piece, k):
        pb[piece, k] = pair(b_rows, piece, k).astype(BF16)
        pair_copy(piece, k).start()

    def pair_own(piece, k):
        own_p[piece, k] = pair(own_rows, piece, k)

    def pair_both(piece, k):
        total = pair(both_rows, piece, k)
        pb[piece, k] = total[b_rows].astype(BF16)
        pair_copy(piece, k).start()
        own_p[piece, k] = total[own_rows]

    norm(opp, na, 0)
    n_copy(0).start()
    for i in (4, 0, 5, 1, 6, 2, 3):
        so[i] = product(na, 0, i).astype(BF16)
        far(i).start()
    norm(a_at, na, BLOCK)
    n_copy(1).start()
    w_pass(0)
    w_pass(1)
    norm(b_at, nl, 0)
    for i in range(FAR_A, RING):
        s_b[i] = product(nl, 0, i).astype(BF16)
        to_b(i).start()
    for i in range(FAR_A):
        s_a[i] = product(na, BLOCK, i).astype(BF16)
        to_a(i).start()
    w_pass(2)
    norm(y, nl, BLOCK)
    for i in range(RING):
        own_r[i] = product(nl, BLOCK, i)
    n_copy(0).wait_recv()
    beside_piece = CORES * x_at + 1 - core

    def near_b(k, carry):
        pair_b(near_piece, k)
        w_sibling(0, k).wait_recv()
        pair_b(beside_piece, k)
        return carry

    lax.fori_loop(0, CHUNKS, near_b, 0)
    for i in range(FAR_A):
        ahead = product(nl, 0, i)
        far(i).wait_recv()
        s_b[i] = (ahead + ro[i].astype(F32)).astype(BF16)
        to_b(i).start()
    for i in range(FAR_A, RING):
        ahead = product(na, BLOCK, i)
        far(i).wait_recv()
        s_a[i] = (ahead + ro[i].astype(F32)).astype(BF16)
        to_a(i).start()
    n_copy(1).wait_recv()

    def near_own(k, carry):
        pair_own(near_piece, k)
        pair_own(beside_piece, k)
        return carry

    lax.fori_loop(0, CHUNKS, near_own, 0)

    def side_both(k, carry):
        for side, at in ((0, down), (1, up)):
            w_beside(side, k).wait_recv()
            w_sibling(1 + side, k).start()
        for at in (down, up):
            pair_both(CORES * at + core, k)
        for side, at in ((0, down), (1, up)):
            w_sibling(1 + side, k).wait_recv()
            pair_both(CORES * at + 1 - core, k)
        return carry

    lax.fori_loop(0, CHUNKS, side_both, 0)

    def finish(piece, k):
        pair_copy(piece, k).wait_recv()
        ob[:, pl.ds(column(piece, k), LANES)] = (own_p[piece, k] + rb[piece, k].astype(F32)).astype(BF16)

    def near_last(k, carry):
        finish(near_piece, k)
        finish(beside_piece, k)
        return carry

    lax.fori_loop(0, CHUNKS, near_last, 0)
    for i in range(RING):
        to_a(i).wait_recv()
        to_b(i).wait_recv()
        ob[:, ring_columns(i)] = (own_r[i] + rf_a[i].astype(F32) + rf_b[i].astype(F32)).astype(BF16)

    def side_last(k, carry):
        for c in range(CORES):
            for at in (down, up):
                finish(CORES * at + lax.rem(core + c, CORES), k)
        return carry

    lax.fori_loop(0, CHUNKS, side_last, 0)

    core_log.wait_send()
    core_state.wait_send()
    for j in range(X):
        core_back(j).wait_send()
    for j in range(1, X):
        for copy in x_copies(j):
            copy.wait_send()
        back_copy(j).wait_send()
    for j in range(1, GROUP):
        pl.when(z_in + j < GROUP)(functools.partial(z_sent, j))

    @pl.when(z == gate_z)
    def _():
        for j in range(z_n - GROUP):
            gate_copy(j, GROUP + j).wait_send()

    for i in range(RING):
        far(i).wait_send()
        to_a(i).wait_send()
        to_b(i).wait_send()
    n_copy(0).wait_send()
    n_copy(1).wait_send()

    def drain(k, carry):
        w_first(k).wait_send()
        for side in range(2):
            w_beside(side, k).wait_send()
        for source, at in enumerate((x_at, down, up)):
            w_sibling(source, k).wait_send()
            for c in range(CORES):
                pair_copy(CORES * at + c, k).wait_send()
        return carry

    lax.fori_loop(0, CHUNKS, drain, 0)


def solution(mesh):
    y_n = mesh.shape["head"]
    z_n = mesh.shape["seq"] // ROW

    def per_device(x, g, sr, dl, b, c, sk, ng, w):
        tokens, width = x.shape
        heads = dl.shape[0]
        dout = w.shape[1]
        blocks = tokens // BLOCK
        pieces = X * CORES
        slab = N // ROW
        hbm_spec = pl.BlockSpec(memory_space=pltpu.HBM)
        vmem_spec = pl.BlockSpec(memory_space=pltpu.VMEM)
        dma = pltpu.SemaphoreType.DMA
        vmem = pltpu.VMEM
        ring = (RING, BLOCK, PIECE)
        chunks = (pieces, CHUNKS, BLOCK, LANES)
        normed = (2 * BLOCK, width)
        rows = (X, slab, width)
        log = (8, LANES)
        return pl.pallas_call(
            functools.partial(kernel, z_n, y_n),
            out_shape=jax.ShapeDtypeStruct((tokens // y_n, dout), BF16),
            in_specs=[hbm_spec] * 3 + [vmem_spec] + [hbm_spec] * 2 + [vmem_spec] * 2 + [hbm_spec],
            out_specs=vmem_spec,
            scratch_shapes=[
                vmem((tokens, width), F32), vmem((tokens, width), BF16), vmem((heads, tokens), F32),
                vmem((tokens, N), F32), vmem((tokens, N), F32), vmem(w.shape, BF16),
                vmem((heads, width), BF16), vmem((4, 4 * heads, width), BF16), vmem((blocks, heads, BLOCK), F32),
                vmem((blocks, BLOCK, 4 * heads), F32), vmem((blocks, BLOCK, 4 * heads), BF16),
                vmem((blocks, N, BLOCK), BF16), vmem((tokens, N), BF16),
                vmem((blocks, N, width), F32), vmem((blocks, 8, width), F32),
                vmem((CORES,) + rows, BF16), vmem((CORES,) + rows, BF16),
                vmem(rows, BF16), vmem(rows, BF16), vmem(rows, BF16), vmem(rows, BF16), vmem(rows, BF16),
                vmem((CORES,) + rows, BF16),
                vmem((slab, width), BF16), vmem((GROUP, slab, width), BF16),
                vmem((slab, width), BF16), vmem((slab, width), BF16),
                vmem(log, F32), vmem((CORES,) + log, F32), vmem(log, F32), vmem((X,) + log, F32),
                vmem(log, F32), vmem((GROUP,) + log, F32), vmem(rows, F32), vmem((slab, width), F32),
                vmem((tokens, width), F32), vmem((tokens, width), F32),
                vmem(normed, BF16), vmem(normed, BF16), vmem(normed, BF16), vmem(ring, F32), vmem(chunks, F32),
                vmem(ring, BF16), vmem(ring, BF16), vmem(ring, BF16), vmem(ring, BF16), vmem(ring, BF16), vmem(ring, BF16),
                vmem(chunks, BF16), vmem(chunks, BF16), vmem((pieces, CHUNKS, width, LANES), BF16),
                dma((6,)), dma((2 + X,)), dma((2 + X,)), dma((X,)), dma((X,)), dma((X,)), dma((X,)),
                dma((GROUP,)), dma((GROUP,)), dma((GROUP,)), dma((GROUP,)),
                dma((z_n - GROUP,)), dma((1,)), dma((X,)), dma((X,)),
                dma((3 * RING,)), dma((3 * RING,)), dma((2,)), dma((2,)), dma((pieces * CHUNKS,)), dma((pieces * CHUNKS,)),
                dma((CHUNKS,)), dma((CHUNKS,)), dma((2 * CHUNKS,)), dma((2 * CHUNKS,)),
                dma((3 * CHUNKS,)), dma((3 * CHUNKS,)),
            ],
            compiler_params=pltpu.CompilerParams(
                collective_id=0, has_side_effects=True, vmem_limit_bytes=58 * 1024 * 1024
            ),
        )(
            x, g, sr.T, dl.reshape(1, heads), b.reshape(tokens, N), c.reshape(tokens, N),
            sk.reshape(1, heads), ng.reshape(1, width), w,
        )

    in_specs = (
        P("seq", "head"), P("seq", "head"), P("seq", "head"), P("head"), P("seq", "head", None),
        P("seq", "head", None), P("head"), P("head"), P("head", None),
    )
    return jax.shard_map(
        per_device, mesh=mesh, in_specs=in_specs, out_specs=P(("seq", "head"), None), check_vma=False
    )
```

```python
import functools

import jax
import jax.numpy as jnp
from jax import lax
from jax.experimental import pallas as pl
from jax.experimental.pallas import tpu as pltpu
from jax.sharding import PartitionSpec as P

F32, BF16 = jnp.float32, jnp.bfloat16
P_SIZE = 64
N = 128
BLOCK = 128
CORES = 2
X = 4
ROW = CORES * X
GROUP = 4
CHUNKS = 3
RING = 7
FAR_A = 4
PIECE = 256
LANES = 128
EXACT = lax.Precision.HIGHEST
MESH = pl.DeviceIdType.MESH


def dot(a, b):
    return jnp.dot(a, b, preferred_element_type=F32)


def exact_dot(a, b):
    return jnp.dot(a, b, preferred_element_type=F32, precision=EXACT)


def stack_rows(rows, count):
    where_row = lax.broadcasted_iota(jnp.int32, (count, rows[0].shape[1]), 0)
    out = jnp.zeros((count, rows[0].shape[1]), F32)
    for k, row in enumerate(rows):
        out = jnp.where(where_row == k, jnp.broadcast_to(row, out.shape), out)
    return out


def kernel(
    z_n, y_n,
    x_hbm, g_hbm, sr_hbm, dl_ref, b_hbm, c_hbm, sk_ref, ng_ref, w_hbm,
    ob,
    xv, gv, srv, bv, cv, wv,
    spread, spread_col, cum_t, cols_s, cols_b, b_t, c_b,
    sent, lead, sbuf, cbuf, xs, xr, bs, br, cs, ubuf, zs, zr, ps, pr,
    lt, cl, xt, xl, zt, zl, pre, zin,
    yw, sg, nl, na, nq, own_r, own_p,
    so, s_a, s_b, ro, rf_a, rf_b, pb, rb, wp,
    in_sem, core_s, core_r, x_s, x_r, xlog_s, xlog_r, z_s, z_r, zlog_s, zlog_r, p_s, p_r, back_s, back_r, sum_s, sum_r,
    n_s, n_r, pair_s, pair_r, wa_s, wa_r, wx_s, wx_r, ws_s, ws_r,
):
    tokens, width = xv.shape
    heads = srv.shape[0]
    blocks = tokens // BLOCK
    slab = N // ROW
    me = lax.axis_index("seq")
    y = lax.axis_index("head")
    z, r = lax.div(me, ROW), lax.rem(me, ROW)
    x_at, core = lax.div(r, CORES), lax.rem(r, CORES)
    z_in = lax.rem(z, GROUP)
    a_at, b_at, opp = y + 1 - 2 * lax.rem(y, 2), y_n - 1 - y, lax.rem(y + 2, y_n)
    sibling = (me + 1 - 2 * core, y)
    gate_z = GROUP - 1

    def x_peer(j):
        return lax.rem(x_at + j, X)

    def at_x(k):
        return (z * ROW + k * CORES + core, y)

    def at_z(k):
        return (k * ROW + r, y)

    barrier = pltpu.get_barrier_semaphore()

    def greet(where):
        pl.semaphore_signal(barrier, inc=1, device_id=where, device_id_type=MESH)

    greet(sibling)
    for j in range(1, X):
        greet(at_x(x_peer(j)))
    greet((me, a_at))
    greet((me, b_at))
    for j in range(1, GROUP):
        pl.when(z_in >= j)(functools.partial(greet, at_z(z - j)))
    pl.when(z >= GROUP)(functools.partial(greet, at_z(gate_z)))

    loads = [
        pltpu.make_async_copy(src, dst, in_sem.at[k])
        for k, (src, dst) in enumerate(
            ((sr_hbm, srv), (b_hbm, bv), (x_hbm, xv), (c_hbm, cv), (g_hbm, gv), (w_hbm, wv))
        )
    ]
    for load in loads[:3]:
        load.start()

    head_of = lax.broadcasted_iota(jnp.int32, (heads, width), 1) // P_SIZE
    spread[...] = jnp.where(head_of == lax.broadcasted_iota(jnp.int32, (heads, width), 0), 1.0, 0.0).astype(BF16)
    spread_col[...] = jnp.zeros(spread_col.shape, BF16)
    for k in range(1, 4):
        spread_col[k, k * heads : (k + 1) * heads, :] = spread[...]

    def spread_rows(rows):
        high = rows.astype(BF16)
        return dot(high, spread[...]) + dot((rows - high.astype(F32)).astype(BF16), spread[...])

    def tile_of(row):
        return jnp.concatenate([row, jnp.zeros((1, LANES - heads), F32)], axis=1)

    loads[0].wait()
    rate = jnp.transpose(jnp.broadcast_to(jnp.exp(dl_ref[...]), (BLOCK, heads)))
    row_i = lax.broadcasted_iota(jnp.int32, (BLOCK, BLOCK), 0)
    col_i = lax.broadcasted_iota(jnp.int32, (BLOCK, BLOCK), 1)
    upper = jnp.where(row_i <= col_i, 1.0, 0.0)
    totals, leads = [], []
    so_far = jnp.zeros((1, heads), F32)
    for c in range(blocks):
        raw = srv[:, c * BLOCK : (c + 1) * BLOCK]
        step = jnp.maximum(raw, 0.0) + jnp.log1p(jnp.exp(-jnp.abs(raw)))
        cum = exact_dot(-step * rate, upper)
        cum_t[c] = cum
        to_end = step * jnp.exp(cum[:, BLOCK - 1 : BLOCK] - cum)
        cols = jnp.transpose(jnp.concatenate([cum, to_end, jnp.exp(cum), step], axis=0))
        cols_s[c] = cols
        cols_b[c] = cols.astype(BF16)
        total = cols[BLOCK - 1 : BLOCK, 0:heads]
        totals.append(total)
        leads.append(so_far)
        so_far = so_far + total
    lt[...] = jnp.zeros(lt.shape, F32)
    lt[:, 0:heads] = jnp.broadcast_to(so_far, (8, heads))
    factors = spread_rows(jnp.exp(stack_rows(totals + leads, 8)))
    for c in range(blocks):
        lead[c] = jnp.broadcast_to(factors[blocks + c : blocks + c + 1], (8, width))

    loads[1].wait()
    for c in range(blocks):
        b_t[c] = jnp.transpose(bv[c * BLOCK : (c + 1) * BLOCK, :]).astype(BF16)
    loads[2].wait()
    for load in loads[3:]:
        load.start()
    pl.semaphore_wait(barrier, X + 2 + (GROUP - 1 - z_in) + jnp.where(z == gate_z, z_n - GROUP, 0))

    up, down = x_peer(1), x_peer(X - 1)
    near_piece = CORES * x_at + core

    def column(piece, k):
        quarter = lax.div(piece, CORES) * (wv.shape[1] // X)
        return pl.multiple_of(quarter + lax.rem(piece, CORES) * CHUNKS * LANES + k * LANES, LANES)

    def w_first(k):
        return pltpu.make_async_remote_copy(
            w_hbm.at[:, pl.ds(column(near_piece, k), LANES)], wp.at[near_piece, k], wa_s.at[k], wa_r.at[k],
            device_id=(me, a_at), device_id_type=MESH,
        )

    def w_beside(side, k):
        return pltpu.make_async_remote_copy(
            wp.at[near_piece, k], wp.at[near_piece, k], wx_s.at[side * CHUNKS + k], wx_r.at[side * CHUNKS + k],
            device_id=at_x(up if side == 0 else down), device_id_type=MESH,
        )

    def w_sibling(source, k):
        piece = CORES * (x_at, down, up)[source] + core
        return pltpu.make_async_remote_copy(
            wp.at[piece, k], wp.at[piece, k], ws_s.at[source * CHUNKS + k], ws_r.at[source * CHUNKS + k],
            device_id=sibling, device_id_type=MESH,
        )

    def w_pass(k):
        w_first(k).wait_recv()
        w_beside(0, k).start()
        w_beside(1, k).start()
        w_sibling(0, k).start()

    for k in range(CHUNKS):
        w_first(k).start()

    tile = 256
    for t in range(width // tile):
        lanes = slice(t * tile, (t + 1) * tile)
        state = jnp.zeros((N, tile), F32)
        for c in range(blocks):
            rows = slice(c * BLOCK, (c + 1) * BLOCK)
            sent[c, :, lanes] = state
            ended = (xv[rows, lanes] * dot(cols_b[c], spread_col[1, :, lanes])).astype(BF16)
            state = state * factors[c : c + 1, lanes] + dot(b_t[c], ended)
        sbuf[:, :, :, lanes] = state.astype(BF16).reshape(CORES, X, slab, tile)

    core_log = pltpu.make_async_remote_copy(
        lt, cl.at[core], core_s.at[0], core_r.at[0], device_id=sibling, device_id_type=MESH
    )
    core_state = pltpu.make_async_remote_copy(
        sbuf.at[1 - core], cbuf.at[core], core_s.at[1], core_r.at[1], device_id=sibling, device_id_type=MESH
    )
    core_log.start()
    core_state.start()
    cl[core] = lt[...]
    cbuf[core] = sbuf[core]
    core_log.wait_recv()
    log_first, log_second = cl[0][0:1, 0:heads], cl[1][0:1, 0:heads]
    decay_core = spread_rows(jnp.exp(stack_rows([log_first, log_second], 8)))
    xt[...] = cl[0] + cl[1]
    core_state.wait_recv()
    for k in range(X):
        xs[k] = (cbuf[0, k].astype(F32) * decay_core[1:2] + cbuf[1, k].astype(F32)).astype(BF16)

    def x_copies(j):
        k = x_peer(j)
        return (
            pltpu.make_async_remote_copy(
                xt, xl.at[x_at], xlog_s.at[j], xlog_r.at[j], device_id=at_x(k), device_id_type=MESH
            ),
            pltpu.make_async_remote_copy(
                xs.at[k], xr.at[x_at], x_s.at[j], x_r.at[j], device_id=at_x(k), device_id_type=MESH
            ),
        )

    for j in (2, 1, 3):
        for copy in x_copies(j):
            copy.start()
    xl[x_at] = xt[...]
    xr[x_at] = xs[x_at]

    first_half = lax.broadcasted_iota(jnp.int32, (BLOCK, LANES), 1) < P_SIZE
    loads[3].wait()
    c_b[...] = cv[...].astype(BF16)
    loads[4].wait()
    skip = spread_rows(jnp.broadcast_to(sk_ref[...], (8, heads)))

    def within(c, carry):
        rows = pl.ds(pl.multiple_of(c * BLOCK, BLOCK), BLOCK)
        scores = jnp.where(row_i >= col_i, dot(c_b[rows, :], b_t[c]), 0.0)
        cum = cols_s[c]
        across = cum_t[c]
        cols = cols_b[c]
        for pair in range(width // LANES):
            lanes = slice(pair * LANES, (pair + 1) * LANES)
            mixes = []
            for h in (2 * pair, 2 * pair + 1):
                gap = jnp.minimum(cum[:, h : h + 1] - across[h : h + 1, :], 0.0)
                mixes.append((scores * jnp.exp(gap)).astype(BF16))
            x = xv[rows, lanes]
            weighted = x * dot(cols, spread_col[3, :, lanes])
            both = jnp.concatenate(
                [jnp.where(first_half, weighted, 0.0), jnp.where(first_half, 0.0, weighted)], axis=0
            ).astype(BF16)
            yw[rows, lanes] = dot(jnp.concatenate(mixes, axis=1), both) + skip[0:1, lanes] * x
            gate = gv[rows, lanes].astype(F32)
            sg[rows, lanes] = gate / (1.0 + jnp.exp(-gate))
        return carry

    lax.fori_loop(0, blocks - 1, within, 0)

    for j in range(1, X):
        for copy in x_copies(j):
            copy.wait_recv()
    logs = [xl[k][0:1, 0:heads] for k in range(X)]
    ahead, running = [], jnp.zeros((1, heads), F32)
    for log in logs:
        ahead.append(running)
        running = running + log
    decay_row = spread_rows(jnp.exp(stack_rows(logs + ahead, 8)))
    state = jnp.zeros((slab, width), F32)
    for k in range(X):
        pre[k] = state
        state = state * decay_row[k : k + 1] + xr[k].astype(F32)
    zs[...] = state.astype(BF16)
    zt[...] = jnp.zeros(zt.shape, F32)
    zt[:, 0:heads] = jnp.broadcast_to(running, (8, heads))

    def z_copies(j, to):
        return (
            pltpu.make_async_remote_copy(
                zt, zl.at[z_in], zlog_s.at[j], zlog_r.at[j], device_id=at_z(to), device_id_type=MESH
            ),
            pltpu.make_async_remote_copy(
                zs, zr.at[z_in], z_s.at[j], z_r.at[j], device_id=at_z(to), device_id_type=MESH
            ),
        )

    def z_send(j):
        for copy in z_copies(j, z + j):
            copy.start()

    def z_take(j):
        for copy in z_copies(j, z):
            copy.wait_recv()

    def z_sent(j):
        for copy in z_copies(j, z + j):
            copy.wait_send()

    for j in range(1, GROUP):
        pl.when(z_in + j < GROUP)(functools.partial(z_send, j))

    def join_z():
        for j in range(1, GROUP):
            pl.when(z_in >= j)(functools.partial(z_take, j))
        logs, before = [], jnp.zeros((1, heads), F32)
        for k in range(GROUP - 1):
            log = jnp.where(k < z_in, zl[k][0:1, 0:heads], 0.0)
            logs.append(log)
            before = before + log
        decay_z = spread_rows(jnp.exp(stack_rows(logs + [before, running], 8)))
        zin[...] = jnp.zeros(zin.shape, F32)
        for k in range(GROUP - 1):

            @pl.when(k < z_in)
            def _(k=k):
                zin[...] = zin[...] * decay_z[k : k + 1] + zr[k].astype(F32)

        return decay_z

    def gate_copy(j, to):
        return pltpu.make_async_remote_copy(ps, pr, p_s.at[j], p_r.at[0], device_id=at_z(to), device_id_type=MESH)

    @pl.when(z == gate_z)
    def _():
        decay_z = join_z()
        ps[...] = (zin[...] * decay_z[GROUP : GROUP + 1] + state).astype(BF16)
        for j in range(z_n - GROUP - 1, -1, -1):
            gate_copy(j, GROUP + j).start()

    lax.fori_loop(blocks - 1, blocks, within, 0)

    @pl.when(z != gate_z)
    def _():
        decay_z = join_z()

        @pl.when(z >= GROUP)
        def _():
            gate_copy(0, z).wait_recv()
            zin[...] = zin[...] + pr[...].astype(F32) * decay_z[GROUP - 1 : GROUP]

    for k in range(X):
        bs[k] = (pre[k] + zin[...] * decay_row[X + k : X + k + 1]).astype(BF16)

    def back_copy(j):
        k = x_peer(j)
        return pltpu.make_async_remote_copy(
            bs.at[k], br.at[x_at], back_s.at[j], back_r.at[j], device_id=at_x(k), device_id_type=MESH
        )

    def core_back(j):
        k = lax.rem(x_at + X - j, X)
        return pltpu.make_async_remote_copy(
            cs.at[k], ubuf.at[core, k], core_s.at[2 + j], core_r.at[2 + j], device_id=sibling, device_id_type=MESH
        )

    for j in (2, 1, 3):
        back_copy(j).start()
    br[x_at] = bs[x_at]
    loads[5].wait()
    for j in (0, 1, 3, 2):
        if j:
            back_copy(j).wait_recv()
        k = lax.rem(x_at + X - j, X)
        came = br[k]
        passed = (came.astype(F32) * decay_core[0:1] + cbuf[0, k].astype(F32)).astype(BF16)
        cs[k] = jnp.where(core == 0, passed, came)
        ubuf[core, k] = jnp.where(core == 0, came, passed)
        core_back(j).start()
    for j in range(X):
        core_back(j).wait_recv()

    def norm(d, into, at):
        rows = pl.ds(pl.multiple_of(d * BLOCK, BLOCK), BLOCK)
        led = lead[d]
        squares = jnp.zeros((BLOCK, 1), F32)
        c_rows = c_b[rows, :]
        cols = cols_b[d]
        for t in range(width // tile):
            lanes = slice(t * tile, (t + 1) * tile)
            came = ubuf[:, :, :, lanes].reshape(N, tile).astype(F32)
            entering = (sent[d, :, lanes] + led[0:1, lanes] * came).astype(BF16)
            ssd = yw[rows, lanes] + dot(c_rows, entering) * dot(cols, spread_col[2, :, lanes])
            gated = ssd * sg[rows, lanes]
            squares = squares + jnp.sum(gated * gated, axis=1, keepdims=True)
            sg[rows, lanes] = gated
        scale = lax.rsqrt(squares * (1.0 / width) + 1e-05)
        for t in range(width // tile):
            lanes = slice(t * tile, (t + 1) * tile)
            into[at : at + BLOCK, lanes] = (sg[rows, lanes] * scale * ng_ref[:, lanes]).astype(BF16)

    def ring_columns(i):
        quarter = wv.shape[1] // X
        if i < X:
            start = x_peer(2) * quarter + i * PIECE
        else:
            start = x_peer((0, 1, X - 1)[i - X]) * quarter + CORES * CHUNKS * LANES
        return pl.ds(pl.multiple_of(start, PIECE), PIECE)

    def product(of, at, i):
        return dot(of[at : at + BLOCK, :], wv[:, ring_columns(i)])

    def far(i):
        return pltpu.make_async_remote_copy(
            so.at[i], ro.at[i], sum_s.at[i], sum_r.at[i],
            device_id=(me, a_at if i < FAR_A else b_at), device_id_type=MESH,
        )

    def to_a(i):
        return pltpu.make_async_remote_copy(
            s_a.at[i], rf_a.at[i], sum_s.at[RING + i], sum_r.at[RING + i], device_id=(me, a_at), device_id_type=MESH
        )

    def to_b(i):
        return pltpu.make_async_remote_copy(
            s_b.at[i], rf_b.at[i], sum_s.at[2 * RING + i], sum_r.at[2 * RING + i],
            device_id=(me, b_at), device_id_type=MESH,
        )

    def n_copy(i):
        rows = slice(i * BLOCK, (i + 1) * BLOCK)
        return pltpu.make_async_remote_copy(
            na.at[rows, :], nq.at[rows, :], n_s.at[i], n_r.at[i], device_id=(me, a_at), device_id_type=MESH
        )

    def pair_copy(piece, k):
        where = piece * CHUNKS + k
        return pltpu.make_async_remote_copy(
            pb.at[piece, k], rb.at[piece, k], pair_s.at[where], pair_r.at[where],
            device_id=(me, b_at), device_id_type=MESH,
        )

    def pair(rows, piece, k):
        columns = pl.ds(column(piece, k), LANES)
        return dot(nl[rows, :], wv[:, columns]) + dot(nq[rows, :], wp[piece, k])

    b_rows, own_rows = slice(0, BLOCK), slice(BLOCK, 2 * BLOCK)

    def pair_b(piece, k):
        pb[piece, k] = pair(b_rows, piece, k).astype(BF16)
        pair_copy(piece, k).start()

    def pair_own(piece, k):
        own_p[piece, k] = pair(own_rows, piece, k)

    norm(opp, na, 0)
    n_copy(0).start()
    for i in (4, 0, 5, 1, 6, 2, 3):
        so[i] = product(na, 0, i).astype(BF16)
        far(i).start()
    norm(a_at, na, BLOCK)
    n_copy(1).start()
    w_pass(0)
    w_pass(1)
    norm(b_at, nl, 0)
    for i in range(FAR_A, RING):
        s_b[i] = product(nl, 0, i).astype(BF16)
        to_b(i).start()
    for i in range(FAR_A):
        s_a[i] = product(na, BLOCK, i).astype(BF16)
        to_a(i).start()
    w_pass(2)
    norm(y, nl, BLOCK)
    for i in range(RING):
        own_r[i] = product(nl, BLOCK, i)
    n_copy(0).wait_recv()
    beside_piece = CORES * x_at + 1 - core

    def near_b(k, carry):
        pair_b(near_piece, k)
        w_sibling(0, k).wait_recv()
        pair_b(beside_piece, k)
        return carry

    lax.fori_loop(0, CHUNKS, near_b, 0)
    for i in range(FAR_A):
        ahead = product(nl, 0, i)
        far(i).wait_recv()
        s_b[i] = (ahead + ro[i].astype(F32)).astype(BF16)
        to_b(i).start()
    for i in range(FAR_A, RING):
        ahead = product(na, BLOCK, i)
        far(i).wait_recv()
        s_a[i] = (ahead + ro[i].astype(F32)).astype(BF16)
        to_a(i).start()

    def near_own(k, carry):
        pair_own(near_piece, k)
        pair_own(beside_piece, k)
        return carry

    def side_b(k, carry):
        for side in range(2):
            w_beside(side, k).wait_recv()
            w_sibling(1 + side, k).start()
        for at in (down, up):
            pair_b(CORES * at + core, k)
        for side, at in ((0, down), (1, up)):
            w_sibling(1 + side, k).wait_recv()
            pair_b(CORES * at + 1 - core, k)
        return carry

    def side_own(k, carry):
        for at in (down, up):
            for c in range(CORES):
                pair_own(CORES * at + c, k)
        return carry

    lax.fori_loop(0, CHUNKS - 1, side_b, 0)
    n_copy(1).wait_recv()
    lax.fori_loop(0, CHUNKS, near_own, 0)
    lax.fori_loop(CHUNKS - 1, CHUNKS, side_b, 0)
    lax.fori_loop(0, CHUNKS, side_own, 0)

    def finish(piece, k):
        pair_copy(piece, k).wait_recv()
        ob[:, pl.ds(column(piece, k), LANES)] = (own_p[piece, k] + rb[piece, k].astype(F32)).astype(BF16)

    def near_last(k, carry):
        finish(near_piece, k)
        finish(beside_piece, k)
        return carry

    lax.fori_loop(0, CHUNKS, near_last, 0)
    for i in range(RING):
        to_a(i).wait_recv()
        to_b(i).wait_recv()
        ob[:, ring_columns(i)] = (own_r[i] + rf_a[i].astype(F32) + rf_b[i].astype(F32)).astype(BF16)

    def side_last(k, carry):
        for c in range(CORES):
            for at in (down, up):
                finish(CORES * at + lax.rem(core + c, CORES), k)
        return carry

    lax.fori_loop(0, CHUNKS, side_last, 0)

    core_log.wait_send()
    core_state.wait_send()
    for j in range(X):
        core_back(j).wait_send()
    for j in range(1, X):
        for copy in x_copies(j):
            copy.wait_send()
        back_copy(j).wait_send()
    for j in range(1, GROUP):
        pl.when(z_in + j < GROUP)(functools.partial(z_sent, j))

    @pl.when(z == gate_z)
    def _():
        for j in range(z_n - GROUP):
            gate_copy(j, GROUP + j).wait_send()

    for i in range(RING):
        far(i).wait_send()
        to_a(i).wait_send()
        to_b(i).wait_send()
    n_copy(0).wait_send()
    n_copy(1).wait_send()

    def drain(k, carry):
        w_first(k).wait_send()
        for side in range(2):
            w_beside(side, k).wait_send()
        for source, at in enumerate((x_at, down, up)):
            w_sibling(source, k).wait_send()
            for c in range(CORES):
                pair_copy(CORES * at + c, k).wait_send()
        return carry

    lax.fori_loop(0, CHUNKS, drain, 0)


def solution(mesh):
    y_n = mesh.shape["head"]
    z_n = mesh.shape["seq"] // ROW

    def per_device(x, g, sr, dl, b, c, sk, ng, w):
        tokens, width = x.shape
        heads = dl.shape[0]
        dout = w.shape[1]
        blocks = tokens // BLOCK
        pieces = X * CORES
        slab = N // ROW
        hbm_spec = pl.BlockSpec(memory_space=pltpu.HBM)
        vmem_spec = pl.BlockSpec(memory_space=pltpu.VMEM)
        dma = pltpu.SemaphoreType.DMA
        vmem = pltpu.VMEM
        ring = (RING, BLOCK, PIECE)
        chunks = (pieces, CHUNKS, BLOCK, LANES)
        normed = (2 * BLOCK, width)
        rows = (X, slab, width)
        log = (8, LANES)
        return pl.pallas_call(
            functools.partial(kernel, z_n, y_n),
            out_shape=jax.ShapeDtypeStruct((tokens // y_n, dout), BF16),
            in_specs=[hbm_spec] * 3 + [vmem_spec] + [hbm_spec] * 2 + [vmem_spec] * 2 + [hbm_spec],
            out_specs=vmem_spec,
            scratch_shapes=[
                vmem((tokens, width), F32), vmem((tokens, width), BF16), vmem((heads, tokens), F32),
                vmem((tokens, N), F32), vmem((tokens, N), F32), vmem(w.shape, BF16),
                vmem((heads, width), BF16), vmem((4, 4 * heads, width), BF16), vmem((blocks, heads, BLOCK), F32),
                vmem((blocks, BLOCK, 4 * heads), F32), vmem((blocks, BLOCK, 4 * heads), BF16),
                vmem((blocks, N, BLOCK), BF16), vmem((tokens, N), BF16),
                vmem((blocks, N, width), F32), vmem((blocks, 8, width), F32),
                vmem((CORES,) + rows, BF16), vmem((CORES,) + rows, BF16),
                vmem(rows, BF16), vmem(rows, BF16), vmem(rows, BF16), vmem(rows, BF16), vmem(rows, BF16),
                vmem((CORES,) + rows, BF16),
                vmem((slab, width), BF16), vmem((GROUP, slab, width), BF16),
                vmem((slab, width), BF16), vmem((slab, width), BF16),
                vmem(log, F32), vmem((CORES,) + log, F32), vmem(log, F32), vmem((X,) + log, F32),
                vmem(log, F32), vmem((GROUP,) + log, F32), vmem(rows, F32), vmem((slab, width), F32),
                vmem((tokens, width), F32), vmem((tokens, width), F32),
                vmem(normed, BF16), vmem(normed, BF16), vmem(normed, BF16), vmem(ring, F32), vmem(chunks, F32),
                vmem(ring, BF16), vmem(ring, BF16), vmem(ring, BF16), vmem(ring, BF16), vmem(ring, BF16), vmem(ring, BF16),
                vmem(chunks, BF16), vmem(chunks, BF16), vmem((pieces, CHUNKS, width, LANES), BF16),
                dma((6,)), dma((2 + X,)), dma((2 + X,)), dma((X,)), dma((X,)), dma((X,)), dma((X,)),
                dma((GROUP,)), dma((GROUP,)), dma((GROUP,)), dma((GROUP,)),
                dma((z_n - GROUP,)), dma((1,)), dma((X,)), dma((X,)),
                dma((3 * RING,)), dma((3 * RING,)), dma((2,)), dma((2,)), dma((pieces * CHUNKS,)), dma((pieces * CHUNKS,)),
                dma((CHUNKS,)), dma((CHUNKS,)), dma((2 * CHUNKS,)), dma((2 * CHUNKS,)),
                dma((3 * CHUNKS,)), dma((3 * CHUNKS,)),
            ],
            compiler_params=pltpu.CompilerParams(
                collective_id=0, has_side_effects=True, vmem_limit_bytes=58 * 1024 * 1024
            ),
        )(
            x, g, sr.T, dl.reshape(1, heads), b.reshape(tokens, N), c.reshape(tokens, N),
            sk.reshape(1, heads), ng.reshape(1, width), w,
        )

    in_specs = (
        P("seq", "head"), P("seq", "head"), P("seq", "head"), P("head"), P("seq", "head", None),
        P("seq", "head", None), P("head"), P("head"), P("head", None),
    )
    return jax.shard_map(
        per_device, mesh=mesh, in_specs=in_specs, out_specs=P(("seq", "head"), None), check_vma=False
    )
```

```python
import functools

import jax
import jax.numpy as jnp
from jax import lax
from jax.experimental import pallas as pl
from jax.experimental.pallas import tpu as pltpu
from jax.sharding import PartitionSpec as P

F32, BF16 = jnp.float32, jnp.bfloat16
P_SIZE = 64
N = 128
BLOCK = 128
CORES = 2
X = 4
ROW = CORES * X
GROUP = 4
CHUNKS = 3
RING = 7
FAR_A = 4
PIECE = 256
LANES = 128
EXACT = lax.Precision.HIGHEST
MESH = pl.DeviceIdType.MESH


def dot(a, b):
    return jnp.dot(a, b, preferred_element_type=F32)


def exact_dot(a, b):
    return jnp.dot(a, b, preferred_element_type=F32, precision=EXACT)


def stack_rows(rows, count):
    where_row = lax.broadcasted_iota(jnp.int32, (count, rows[0].shape[1]), 0)
    out = jnp.zeros((count, rows[0].shape[1]), F32)
    for k, row in enumerate(rows):
        out = jnp.where(where_row == k, jnp.broadcast_to(row, out.shape), out)
    return out


def kernel(
    z_n, y_n,
    x_hbm, g_hbm, sr_hbm, dl_ref, b_hbm, c_hbm, sk_ref, ng_ref, w_hbm,
    ob,
    xv, gv, srv, bv, cv, wv,
    spread, spread_col, cum_t, cols_s, cols_b, b_t, c_b,
    sent, lead, sbuf, cbuf, xs, xr, bs, br, cs, ubuf, zs, zr, ps, pr,
    lt, cl, xt, xl, zt, zl, pre, zin,
    yw, sg, nl, na, nq, own_r, own_p,
    so, s_a, s_b, ro, rf_a, rf_b, pb, rb, wp,
    in_sem, core_s, core_r, x_s, x_r, xlog_s, xlog_r, z_s, z_r, zlog_s, zlog_r, p_s, p_r, back_s, back_r, sum_s, sum_r,
    n_s, n_r, pair_s, pair_r, wa_s, wa_r, wx_s, wx_r, ws_s, ws_r,
):
    tokens, width = xv.shape
    heads = srv.shape[0]
    blocks = tokens // BLOCK
    slab = N // ROW
    me = lax.axis_index("seq")
    y = lax.axis_index("head")
    z, r = lax.div(me, ROW), lax.rem(me, ROW)
    x_at, core = lax.div(r, CORES), lax.rem(r, CORES)
    z_in = lax.rem(z, GROUP)
    a_at, b_at, opp = y + 1 - 2 * lax.rem(y, 2), y_n - 1 - y, lax.rem(y + 2, y_n)
    sibling = (me + 1 - 2 * core, y)
    gate_z = GROUP - 1

    def x_peer(j):
        return lax.rem(x_at + j, X)

    def at_x(k):
        return (z * ROW + k * CORES + core, y)

    def at_z(k):
        return (k * ROW + r, y)

    barrier = pltpu.get_barrier_semaphore()

    def greet(where):
        pl.semaphore_signal(barrier, inc=1, device_id=where, device_id_type=MESH)

    greet(sibling)
    for j in range(1, X):
        greet(at_x(x_peer(j)))
    greet((me, a_at))
    greet((me, b_at))
    for j in range(1, GROUP):
        pl.when(z_in >= j)(functools.partial(greet, at_z(z - j)))
    pl.when(z >= GROUP)(functools.partial(greet, at_z(gate_z)))

    loads = [
        pltpu.make_async_copy(src, dst, in_sem.at[k])
        for k, (src, dst) in enumerate(
            ((sr_hbm, srv), (b_hbm, bv), (x_hbm, xv), (c_hbm, cv), (g_hbm, gv), (w_hbm, wv))
        )
    ]
    for load in loads[:3]:
        load.start()

    head_of = lax.broadcasted_iota(jnp.int32, (heads, width), 1) // P_SIZE
    spread[...] = jnp.where(head_of == lax.broadcasted_iota(jnp.int32, (heads, width), 0), 1.0, 0.0).astype(BF16)
    spread_col[...] = jnp.zeros(spread_col.shape, BF16)
    for k in range(1, 4):
        spread_col[k, k * heads : (k + 1) * heads, :] = spread[...]

    def spread_rows(rows):
        high = rows.astype(BF16)
        return dot(high, spread[...]) + dot((rows - high.astype(F32)).astype(BF16), spread[...])

    def tile_of(row):
        return jnp.concatenate([row, jnp.zeros((1, LANES - heads), F32)], axis=1)

    loads[0].wait()
    rate = jnp.transpose(jnp.broadcast_to(jnp.exp(dl_ref[...]), (BLOCK, heads)))
    row_i = lax.broadcasted_iota(jnp.int32, (BLOCK, BLOCK), 0)
    col_i = lax.broadcasted_iota(jnp.int32, (BLOCK, BLOCK), 1)
    upper = jnp.where(row_i <= col_i, 1.0, 0.0)
    totals, leads = [], []
    so_far = jnp.zeros((1, heads), F32)
    for c in range(blocks):
        raw = srv[:, c * BLOCK : (c + 1) * BLOCK]
        step = jnp.maximum(raw, 0.0) + jnp.log1p(jnp.exp(-jnp.abs(raw)))
        cum = exact_dot(-step * rate, upper)
        cum_t[c] = cum
        to_end = step * jnp.exp(cum[:, BLOCK - 1 : BLOCK] - cum)
        cols = jnp.transpose(jnp.concatenate([cum, to_end, jnp.exp(cum), step], axis=0))
        cols_s[c] = cols
        cols_b[c] = cols.astype(BF16)
        total = cols[BLOCK - 1 : BLOCK, 0:heads]
        totals.append(total)
        leads.append(so_far)
        so_far = so_far + total
    lt[...] = jnp.zeros(lt.shape, F32)
    lt[:, 0:heads] = jnp.broadcast_to(so_far, (8, heads))
    factors = spread_rows(jnp.exp(stack_rows(totals + leads, 8)))
    for c in range(blocks):
        lead[c] = jnp.broadcast_to(factors[blocks + c : blocks + c + 1], (8, width))

    loads[1].wait()
    for c in range(blocks):
        b_t[c] = jnp.transpose(bv[c * BLOCK : (c + 1) * BLOCK, :]).astype(BF16)
    loads[2].wait()
    for load in loads[3:]:
        load.start()
    up, down = x_peer(1), x_peer(X - 1)
    near_piece = CORES * x_at + core

    def column(piece, k):
        quarter = lax.div(piece, CORES) * (wv.shape[1] // X)
        return pl.multiple_of(quarter + lax.rem(piece, CORES) * CHUNKS * LANES + k * LANES, LANES)

    def w_first(k):
        return pltpu.make_async_remote_copy(
            w_hbm.at[:, pl.ds(column(near_piece, k), LANES)], wp.at[near_piece, k], wa_s.at[k], wa_r.at[k],
            device_id=(me, a_at), device_id_type=MESH,
        )

    def w_beside(side, k):
        return pltpu.make_async_remote_copy(
            wp.at[near_piece, k], wp.at[near_piece, k], wx_s.at[side * CHUNKS + k], wx_r.at[side * CHUNKS + k],
            device_id=at_x(up if side == 0 else down), device_id_type=MESH,
        )

    def w_sibling(source, k):
        piece = CORES * (x_at, down, up)[source] + core
        return pltpu.make_async_remote_copy(
            wp.at[piece, k], wp.at[piece, k], ws_s.at[source * CHUNKS + k], ws_r.at[source * CHUNKS + k],
            device_id=sibling, device_id_type=MESH,
        )

    def w_pass(k):
        w_first(k).wait_recv()
        w_beside(0, k).start()
        w_beside(1, k).start()
        w_sibling(0, k).start()

    tile = 256
    for t in range(width // tile):
        lanes = slice(t * tile, (t + 1) * tile)
        state = jnp.zeros((N, tile), F32)
        for c in range(blocks):
            rows = slice(c * BLOCK, (c + 1) * BLOCK)
            sent[c, :, lanes] = state
            ended = (xv[rows, lanes] * dot(cols_b[c], spread_col[1, :, lanes])).astype(BF16)
            state = state * factors[c : c + 1, lanes] + dot(b_t[c], ended)
        sbuf[:, :, :, lanes] = state.astype(BF16).reshape(CORES, X, slab, tile)

    pl.semaphore_wait(barrier, X + 2 + (GROUP - 1 - z_in) + jnp.where(z == gate_z, z_n - GROUP, 0))

    core_log = pltpu.make_async_remote_copy(
        lt, cl.at[core], core_s.at[0], core_r.at[0], device_id=sibling, device_id_type=MESH
    )
    core_state = pltpu.make_async_remote_copy(
        sbuf.at[1 - core], cbuf.at[core], core_s.at[1], core_r.at[1], device_id=sibling, device_id_type=MESH
    )
    core_log.start()
    core_state.start()
    for k in range(CHUNKS):
        w_first(k).start()
    cl[core] = lt[...]
    cbuf[core] = sbuf[core]
    core_log.wait_recv()
    log_first, log_second = cl[0][0:1, 0:heads], cl[1][0:1, 0:heads]
    decay_core = spread_rows(jnp.exp(stack_rows([log_first, log_second], 8)))
    xt[...] = cl[0] + cl[1]
    core_state.wait_recv()
    for k in range(X):
        xs[k] = (cbuf[0, k].astype(F32) * decay_core[1:2] + cbuf[1, k].astype(F32)).astype(BF16)

    def x_copies(j):
        k = x_peer(j)
        return (
            pltpu.make_async_remote_copy(
                xt, xl.at[x_at], xlog_s.at[j], xlog_r.at[j], device_id=at_x(k), device_id_type=MESH
            ),
            pltpu.make_async_remote_copy(
                xs.at[k], xr.at[x_at], x_s.at[j], x_r.at[j], device_id=at_x(k), device_id_type=MESH
            ),
        )

    for j in (2, 1, 3):
        for copy in x_copies(j):
            copy.start()
    xl[x_at] = xt[...]
    xr[x_at] = xs[x_at]

    first_half = lax.broadcasted_iota(jnp.int32, (BLOCK, LANES), 1) < P_SIZE
    loads[3].wait()
    c_b[...] = cv[...].astype(BF16)
    loads[4].wait()
    skip = spread_rows(jnp.broadcast_to(sk_ref[...], (8, heads)))

    def within(c, carry):
        rows = pl.ds(pl.multiple_of(c * BLOCK, BLOCK), BLOCK)
        scores = jnp.where(row_i >= col_i, dot(c_b[rows, :], b_t[c]), 0.0)
        cum = cols_s[c]
        across = cum_t[c]
        cols = cols_b[c]
        for pair in range(width // LANES):
            lanes = slice(pair * LANES, (pair + 1) * LANES)
            mixes = []
            for h in (2 * pair, 2 * pair + 1):
                gap = jnp.minimum(cum[:, h : h + 1] - across[h : h + 1, :], 0.0)
                mixes.append((scores * jnp.exp(gap)).astype(BF16))
            x = xv[rows, lanes]
            weighted = x * dot(cols, spread_col[3, :, lanes])
            both = jnp.concatenate(
                [jnp.where(first_half, weighted, 0.0), jnp.where(first_half, 0.0, weighted)], axis=0
            ).astype(BF16)
            yw[rows, lanes] = dot(jnp.concatenate(mixes, axis=1), both) + skip[0:1, lanes] * x
            gate = gv[rows, lanes].astype(F32)
            sg[rows, lanes] = gate / (1.0 + jnp.exp(-gate))
        return carry

    lax.fori_loop(0, blocks - 1, within, 0)

    for j in range(1, X):
        for copy in x_copies(j):
            copy.wait_recv()
    logs = [xl[k][0:1, 0:heads] for k in range(X)]
    ahead, running = [], jnp.zeros((1, heads), F32)
    for log in logs:
        ahead.append(running)
        running = running + log
    decay_row = spread_rows(jnp.exp(stack_rows(logs + ahead, 8)))
    state = jnp.zeros((slab, width), F32)
    for k in range(X):
        pre[k] = state
        state = state * decay_row[k : k + 1] + xr[k].astype(F32)
    zs[...] = state.astype(BF16)
    zt[...] = jnp.zeros(zt.shape, F32)
    zt[:, 0:heads] = jnp.broadcast_to(running, (8, heads))

    def z_copies(j, to):
        return (
            pltpu.make_async_remote_copy(
                zt, zl.at[z_in], zlog_s.at[j], zlog_r.at[j], device_id=at_z(to), device_id_type=MESH
            ),
            pltpu.make_async_remote_copy(
                zs, zr.at[z_in], z_s.at[j], z_r.at[j], device_id=at_z(to), device_id_type=MESH
            ),
        )

    def z_send(j):
        for copy in z_copies(j, z + j):
            copy.start()

    def z_take(j):
        for copy in z_copies(j, z):
            copy.wait_recv()

    def z_sent(j):
        for copy in z_copies(j, z + j):
            copy.wait_send()

    for j in range(1, GROUP):
        pl.when(z_in + j < GROUP)(functools.partial(z_send, j))

    def join_z():
        for j in range(1, GROUP):
            pl.when(z_in >= j)(functools.partial(z_take, j))
        logs, before = [], jnp.zeros((1, heads), F32)
        for k in range(GROUP - 1):
            log = jnp.where(k < z_in, zl[k][0:1, 0:heads], 0.0)
            logs.append(log)
            before = before + log
        decay_z = spread_rows(jnp.exp(stack_rows(logs + [before, running], 8)))
        zin[...] = jnp.zeros(zin.shape, F32)
        for k in range(GROUP - 1):

            @pl.when(k < z_in)
            def _(k=k):
                zin[...] = zin[...] * decay_z[k : k + 1] + zr[k].astype(F32)

        return decay_z

    def gate_copy(j, to):
        return pltpu.make_async_remote_copy(ps, pr, p_s.at[j], p_r.at[0], device_id=at_z(to), device_id_type=MESH)

    @pl.when(z == gate_z)
    def _():
        decay_z = join_z()
        ps[...] = (zin[...] * decay_z[GROUP : GROUP + 1] + state).astype(BF16)
        for j in range(z_n - GROUP - 1, -1, -1):
            gate_copy(j, GROUP + j).start()

    lax.fori_loop(blocks - 1, blocks, within, 0)

    @pl.when(z != gate_z)
    def _():
        decay_z = join_z()

        @pl.when(z >= GROUP)
        def _():
            gate_copy(0, z).wait_recv()
            zin[...] = zin[...] + pr[...].astype(F32) * decay_z[GROUP - 1 : GROUP]

    for k in range(X):
        bs[k] = (pre[k] + zin[...] * decay_row[X + k : X + k + 1]).astype(BF16)

    def back_copy(j):
        k = x_peer(j)
        return pltpu.make_async_remote_copy(
            bs.at[k], br.at[x_at], back_s.at[j], back_r.at[j], device_id=at_x(k), device_id_type=MESH
        )

    def core_back(j):
        k = lax.rem(x_at + X - j, X)
        return pltpu.make_async_remote_copy(
            cs.at[k], ubuf.at[core, k], core_s.at[2 + j], core_r.at[2 + j], device_id=sibling, device_id_type=MESH
        )

    for j in (2, 1, 3):
        back_copy(j).start()
    br[x_at] = bs[x_at]
    loads[5].wait()
    for j in (0, 1, 3, 2):
        if j:
            back_copy(j).wait_recv()
        k = lax.rem(x_at + X - j, X)
        came = br[k]
        passed = (came.astype(F32) * decay_core[0:1] + cbuf[0, k].astype(F32)).astype(BF16)
        cs[k] = jnp.where(core == 0, passed, came)
        ubuf[core, k] = jnp.where(core == 0, came, passed)
        core_back(j).start()
    for j in range(X):
        core_back(j).wait_recv()

    def norm(d, into, at):
        rows = pl.ds(pl.multiple_of(d * BLOCK, BLOCK), BLOCK)
        led = lead[d]
        squares = jnp.zeros((BLOCK, 1), F32)
        c_rows = c_b[rows, :]
        cols = cols_b[d]
        for t in range(width // tile):
            lanes = slice(t * tile, (t + 1) * tile)
            came = ubuf[:, :, :, lanes].reshape(N, tile).astype(F32)
            entering = (sent[d, :, lanes] + led[0:1, lanes] * came).astype(BF16)
            ssd = yw[rows, lanes] + dot(c_rows, entering) * dot(cols, spread_col[2, :, lanes])
            gated = ssd * sg[rows, lanes]
            squares = squares + jnp.sum(gated * gated, axis=1, keepdims=True)
            sg[rows, lanes] = gated
        scale = lax.rsqrt(squares * (1.0 / width) + 1e-05)
        for t in range(width // tile):
            lanes = slice(t * tile, (t + 1) * tile)
            into[at : at + BLOCK, lanes] = (sg[rows, lanes] * scale * ng_ref[:, lanes]).astype(BF16)

    def ring_columns(i):
        quarter = wv.shape[1] // X
        if i < X:
            start = x_peer(2) * quarter + i * PIECE
        else:
            start = x_peer((0, 1, X - 1)[i - X]) * quarter + CORES * CHUNKS * LANES
        return pl.ds(pl.multiple_of(start, PIECE), PIECE)

    def product(of, at, i):
        return dot(of[at : at + BLOCK, :], wv[:, ring_columns(i)])

    def far(i):
        return pltpu.make_async_remote_copy(
            so.at[i], ro.at[i], sum_s.at[i], sum_r.at[i],
            device_id=(me, a_at if i < FAR_A else b_at), device_id_type=MESH,
        )

    def to_a(i):
        return pltpu.make_async_remote_copy(
            s_a.at[i], rf_a.at[i], sum_s.at[RING + i], sum_r.at[RING + i], device_id=(me, a_at), device_id_type=MESH
        )

    def to_b(i):
        return pltpu.make_async_remote_copy(
            s_b.at[i], rf_b.at[i], sum_s.at[2 * RING + i], sum_r.at[2 * RING + i],
            device_id=(me, b_at), device_id_type=MESH,
        )

    def n_copy(i):
        rows = slice(i * BLOCK, (i + 1) * BLOCK)
        return pltpu.make_async_remote_copy(
            na.at[rows, :], nq.at[rows, :], n_s.at[i], n_r.at[i], device_id=(me, a_at), device_id_type=MESH
        )

    def pair_copy(piece, k):
        where = piece * CHUNKS + k
        return pltpu.make_async_remote_copy(
            pb.at[piece, k], rb.at[piece, k], pair_s.at[where], pair_r.at[where],
            device_id=(me, b_at), device_id_type=MESH,
        )

    def pair(rows, piece, k):
        columns = pl.ds(column(piece, k), LANES)
        return dot(nl[rows, :], wv[:, columns]) + dot(nq[rows, :], wp[piece, k])

    b_rows, own_rows = slice(0, BLOCK), slice(BLOCK, 2 * BLOCK)

    def pair_b(piece, k):
        pb[piece, k] = pair(b_rows, piece, k).astype(BF16)
        pair_copy(piece, k).start()

    def pair_own(piece, k):
        own_p[piece, k] = pair(own_rows, piece, k)

    norm(opp, na, 0)
    n_copy(0).start()
    for i in (4, 0, 5, 1, 6, 2, 3):
        so[i] = product(na, 0, i).astype(BF16)
        far(i).start()
    norm(a_at, na, BLOCK)
    n_copy(1).start()
    w_pass(0)
    w_pass(1)
    norm(b_at, nl, 0)
    for i in range(FAR_A, RING):
        s_b[i] = product(nl, 0, i).astype(BF16)
        to_b(i).start()
    for i in range(FAR_A):
        s_a[i] = product(na, BLOCK, i).astype(BF16)
        to_a(i).start()
    w_pass(2)
    norm(y, nl, BLOCK)
    for i in range(RING):
        own_r[i] = product(nl, BLOCK, i)
    n_copy(0).wait_recv()
    beside_piece = CORES * x_at + 1 - core

    def near_b(k, carry):
        pair_b(near_piece, k)
        w_sibling(0, k).wait_recv()
        pair_b(beside_piece, k)
        return carry

    lax.fori_loop(0, CHUNKS, near_b, 0)
    for i in range(FAR_A):
        ahead = product(nl, 0, i)
        far(i).wait_recv()
        s_b[i] = (ahead + ro[i].astype(F32)).astype(BF16)
        to_b(i).start()
    for i in range(FAR_A, RING):
        ahead = product(na, BLOCK, i)
        far(i).wait_recv()
        s_a[i] = (ahead + ro[i].astype(F32)).astype(BF16)
        to_a(i).start()

    def near_own(k, carry):
        pair_own(near_piece, k)
        pair_own(beside_piece, k)
        return carry

    def side_b(k, carry):
        for side in range(2):
            w_beside(side, k).wait_recv()
            w_sibling(1 + side, k).start()
        for at in (down, up):
            pair_b(CORES * at + core, k)
        for side, at in ((0, down), (1, up)):
            w_sibling(1 + side, k).wait_recv()
            pair_b(CORES * at + 1 - core, k)
        return carry

    def side_own(k, carry):
        for at in (down, up):
            for c in range(CORES):
                pair_own(CORES * at + c, k)
        return carry

    lax.fori_loop(0, CHUNKS - 1, side_b, 0)
    n_copy(1).wait_recv()
    lax.fori_loop(0, CHUNKS, near_own, 0)
    lax.fori_loop(CHUNKS - 1, CHUNKS, side_b, 0)
    lax.fori_loop(0, CHUNKS, side_own, 0)

    def finish(piece, k):
        pair_copy(piece, k).wait_recv()
        ob[:, pl.ds(column(piece, k), LANES)] = (own_p[piece, k] + rb[piece, k].astype(F32)).astype(BF16)

    def near_last(k, carry):
        finish(near_piece, k)
        finish(beside_piece, k)
        return carry

    lax.fori_loop(0, CHUNKS, near_last, 0)
    for i in range(RING):
        to_a(i).wait_recv()
        to_b(i).wait_recv()
        ob[:, ring_columns(i)] = (own_r[i] + rf_a[i].astype(F32) + rf_b[i].astype(F32)).astype(BF16)

    def side_last(k, carry):
        for c in range(CORES):
            for at in (down, up):
                finish(CORES * at + lax.rem(core + c, CORES), k)
        return carry

    lax.fori_loop(0, CHUNKS, side_last, 0)

    core_log.wait_send()
    core_state.wait_send()
    for j in range(X):
        core_back(j).wait_send()
    for j in range(1, X):
        for copy in x_copies(j):
            copy.wait_send()
        back_copy(j).wait_send()
    for j in range(1, GROUP):
        pl.when(z_in + j < GROUP)(functools.partial(z_sent, j))

    @pl.when(z == gate_z)
    def _():
        for j in range(z_n - GROUP):
            gate_copy(j, GROUP + j).wait_send()

    for i in range(RING):
        far(i).wait_send()
        to_a(i).wait_send()
        to_b(i).wait_send()
    n_copy(0).wait_send()
    n_copy(1).wait_send()

    def drain(k, carry):
        w_first(k).wait_send()
        for side in range(2):
            w_beside(side, k).wait_send()
        for source, at in enumerate((x_at, down, up)):
            w_sibling(source, k).wait_send()
            for c in range(CORES):
                pair_copy(CORES * at + c, k).wait_send()
        return carry

    lax.fori_loop(0, CHUNKS, drain, 0)


def solution(mesh):
    y_n = mesh.shape["head"]
    z_n = mesh.shape["seq"] // ROW

    def per_device(x, g, sr, dl, b, c, sk, ng, w):
        tokens, width = x.shape
        heads = dl.shape[0]
        dout = w.shape[1]
        blocks = tokens // BLOCK
        pieces = X * CORES
        slab = N // ROW
        hbm_spec = pl.BlockSpec(memory_space=pltpu.HBM)
        vmem_spec = pl.BlockSpec(memory_space=pltpu.VMEM)
        dma = pltpu.SemaphoreType.DMA
        vmem = pltpu.VMEM
        ring = (RING, BLOCK, PIECE)
        chunks = (pieces, CHUNKS, BLOCK, LANES)
        normed = (2 * BLOCK, width)
        rows = (X, slab, width)
        log = (8, LANES)
        return pl.pallas_call(
            functools.partial(kernel, z_n, y_n),
            out_shape=jax.ShapeDtypeStruct((tokens // y_n, dout), BF16),
            in_specs=[hbm_spec] * 3 + [vmem_spec] + [hbm_spec] * 2 + [vmem_spec] * 2 + [hbm_spec],
            out_specs=vmem_spec,
            scratch_shapes=[
                vmem((tokens, width), F32), vmem((tokens, width), BF16), vmem((heads, tokens), F32),
                vmem((tokens, N), F32), vmem((tokens, N), F32), vmem(w.shape, BF16),
                vmem((heads, width), BF16), vmem((4, 4 * heads, width), BF16), vmem((blocks, heads, BLOCK), F32),
                vmem((blocks, BLOCK, 4 * heads), F32), vmem((blocks, BLOCK, 4 * heads), BF16),
                vmem((blocks, N, BLOCK), BF16), vmem((tokens, N), BF16),
                vmem((blocks, N, width), F32), vmem((blocks, 8, width), F32),
                vmem((CORES,) + rows, BF16), vmem((CORES,) + rows, BF16),
                vmem(rows, BF16), vmem(rows, BF16), vmem(rows, BF16), vmem(rows, BF16), vmem(rows, BF16),
                vmem((CORES,) + rows, BF16),
                vmem((slab, width), BF16), vmem((GROUP, slab, width), BF16),
                vmem((slab, width), BF16), vmem((slab, width), BF16),
                vmem(log, F32), vmem((CORES,) + log, F32), vmem(log, F32), vmem((X,) + log, F32),
                vmem(log, F32), vmem((GROUP,) + log, F32), vmem(rows, F32), vmem((slab, width), F32),
                vmem((tokens, width), F32), vmem((tokens, width), F32),
                vmem(normed, BF16), vmem(normed, BF16), vmem(normed, BF16), vmem(ring, F32), vmem(chunks, F32),
                vmem(ring, BF16), vmem(ring, BF16), vmem(ring, BF16), vmem(ring, BF16), vmem(ring, BF16), vmem(ring, BF16),
                vmem(chunks, BF16), vmem(chunks, BF16), vmem((pieces, CHUNKS, width, LANES), BF16),
                dma((6,)), dma((2 + X,)), dma((2 + X,)), dma((X,)), dma((X,)), dma((X,)), dma((X,)),
                dma((GROUP,)), dma((GROUP,)), dma((GROUP,)), dma((GROUP,)),
                dma((z_n - GROUP,)), dma((1,)), dma((X,)), dma((X,)),
                dma((3 * RING,)), dma((3 * RING,)), dma((2,)), dma((2,)), dma((pieces * CHUNKS,)), dma((pieces * CHUNKS,)),
                dma((CHUNKS,)), dma((CHUNKS,)), dma((2 * CHUNKS,)), dma((2 * CHUNKS,)),
                dma((3 * CHUNKS,)), dma((3 * CHUNKS,)),
            ],
            compiler_params=pltpu.CompilerParams(
                collective_id=0, has_side_effects=True, vmem_limit_bytes=58 * 1024 * 1024
            ),
        )(
            x, g, sr.T, dl.reshape(1, heads), b.reshape(tokens, N), c.reshape(tokens, N),
            sk.reshape(1, heads), ng.reshape(1, width), w,
        )

    in_specs = (
        P("seq", "head"), P("seq", "head"), P("seq", "head"), P("head"), P("seq", "head", None),
        P("seq", "head", None), P("head"), P("head"), P("head", None),
    )
    return jax.shard_map(
        per_device, mesh=mesh, in_specs=in_specs, out_specs=P(("seq", "head"), None), check_vma=False
    )
```
